32 devices in a mesh: lat: 4 (over y, x), lon: 8 (over z, core).
Axes of the slice: x: 2, y: 2, z: 4, core: 2. Of those that a mesh axis runs over, the one named last changes fastest.
Arguments:
- grid_state: float32 [48, 120, 384], P('lat', 'lon'), may hold values from -6 to 6
- norm_gain: float32 [2, 384], replicated, may hold values from 0.25 to 1.75
- conv_weight: bfloat16 [2, 3, 3, 384, 384], replicated, may hold values from -0.109375 to 0.109375
- filter_weight: bfloat16 [48, 384, 384], P('lat'), may hold values from -0.3125 to 0.3125
- degree_keep: int32 [48, 48], P('lat', 'lon'), may hold values 0 or 1
Outputs:
- updated: float32 [48, 120, 384], P('lat', 'lon')
The draws below stay inside these ranges and needn't reach their ends.
Inputs may be any that keep to these rules, and one draw needn't show every extreme that they name: degree_keep[l, m] is 0 or 1 for degree l and order m.
All inputs are finite; a program needn't handle non-finite values. No bound on the sum of `degree_keep` on one device may be relied on, other than what follows from the above.
Results may differ from the reference program's by a relative error of at most 0.008.
Values may be sent and summed in bfloat16 or wider, within the bound.
A program may use at most 64 MiB of HBM per device.

```python
import math
import jax
import jax.numpy as jnp
from jax import lax

C = 384
NLAT = 48
NLON = 120
DEGREES = 48


def place_ends(drawn, own_key, smallest, high):
    longest = drawn.shape.index(max(drawn.shape))
    spots = []
    for shift in (0, 1):
        where = [jax.random.randint(jax.random.fold_in(own_key, axis), (), 0, length) for axis, length in enumerate(drawn.shape)]
        where[longest] = (where[longest] + shift) % drawn.shape[longest]
        spots.append(tuple(where))
    return drawn.at[spots[0]].set(smallest).at[spots[1]].set(high)


def steps_of(own_key, dims, shards, smallest, top_value):
    level = 1.0
    for position, blocks in shards:
        draws = jax.random.uniform(jax.random.fold_in(jax.random.fold_in(own_key, 6), position), (blocks,), jnp.float32, smallest / len(shards), top_value / len(shards))
        level = level * jnp.repeat(jnp.exp(draws), dims[position] // blocks).reshape((-1,) + (1,) * (len(dims) - 1 - position))
    return level


def gaussian(stream_key, dims, width, limit, pieces=(), held_as=jnp.bfloat16):
    factor_of = steps_of(stream_key, dims, pieces, -0.22, 0.18) if pieces else 1.0
    array = jax.random.normal(stream_key, dims, jnp.float32) * width * factor_of
    return jnp.minimum(jnp.maximum(array, -limit), limit).astype(held_as)


def setup_inputs(seed: int = 0) -> dict:
    key_of = jax.random.split(jax.random.key(seed), 6)
    grid_state = gaussian(key_of[0], (NLAT, NLON, C), 1.0, 6.0, ((0, 4), (1, 8)), jnp.float32)
    norm_gain = jnp.clip(1.0 + 0.15 * jax.random.normal(key_of[1], (2, C), jnp.float32), 0.25, 1.75)
    conv_weight = gaussian(key_of[2], (2, 3, 3, C, C), (9 * C) ** -0.5, 0.109375)
    filter_weight = gaussian(key_of[3], (DEGREES, C, C), C ** -0.5, 0.3125, ((0, 4),))
    degree_keep = place_ends((jax.random.randint(key_of[4], (DEGREES, DEGREES), 0, 4) < 3).astype(jnp.int32), jax.random.fold_in(key_of[4], 1), 0, 1)
    return {"grid_state": grid_state, "norm_gain": norm_gain, "conv_weight": conv_weight, "filter_weight": filter_weight, "degree_keep": degree_keep}


epsilon = 1e-06

def colatitude(row_index, total_rows, float_type):
    theta_rows = (row_index.astype(float_type) + 0.5) * (math.pi / total_rows)
    return (jnp.cos(theta_rows), jnp.sin(theta_rows))

def legendre_table(orders, cosine, sine_values, amount):
    float_type = cosine.dtype
    order_f = orders.astype(float_type)[:, None]
    order_i = orders.astype(jnp.int32)[:, None]
    column = cosine[None, :]
    log_start = 0.5 * (jnp.log((2.0 * order_f + 1.0) / (4.0 * math.pi)) + jax.scipy.special.gammaln(order_f + 0.5) - jax.scipy.special.gammaln(order_f + 1.0) - 0.5 * math.log(math.pi)) + order_f * jnp.log(sine_values)[None, :]
    sectoral = jnp.exp(log_start)

    def advance(carry, degree):
        before, latest = carry
        degree_f = degree.astype(float_type)
        growth = jnp.sqrt(jnp.maximum(4.0 * degree_f * degree_f - 1.0, 1.0) / jnp.maximum(degree_f * degree_f - order_f * order_f, 1.0))
        prior = degree_f - 1.0
        damping = jnp.sqrt(jnp.maximum(prior * prior - order_f * order_f, 0.0) / jnp.maximum(4.0 * prior * prior - 1.0, 1.0))
        grown = growth * (column * latest - damping * before)
        fresh = jnp.where(degree < order_i, jnp.zeros_like(grown), jnp.where(degree == order_i, sectoral, grown)).astype(float_type)
        return ((latest, fresh), fresh)
    zero_rows = jnp.zeros((orders.shape[0], cosine.shape[0]), float_type)
    _, assoc_basis = lax.scan(advance, (zero_rows, zero_rows), jnp.arange(amount, dtype=jnp.int32), unroll=16)
    return assoc_basis

def forward_table(columns, modes, total_cols, float_type):
    lon_index = columns.astype(jnp.int32)[:, None]
    order_index = jnp.arange(modes, dtype=jnp.int32)[None, :]
    phase = (lon_index * order_index % total_cols).astype(float_type) * (2.0 * math.pi / total_cols)
    factor = 2.0 * math.pi / total_cols
    return jnp.stack([jnp.cos(phase) * factor, -jnp.sin(phase) * factor], axis=2).reshape(columns.shape[0], 2 * modes)

def inverse_table(modes, total_cols, float_type):
    order_index = jnp.arange(modes, dtype=jnp.int32)[:, None]
    lon_index = jnp.arange(total_cols, dtype=jnp.int32)[None, :]
    phase = (lon_index * order_index % total_cols).astype(float_type) * (2.0 * math.pi / total_cols)
    factor = jnp.where(order_index == 0, 1.0, 2.0).astype(float_type)
    return jnp.stack([jnp.cos(phase) * factor, -jnp.sin(phase) * factor], axis=1).reshape(2 * modes, total_cols)

def reference(grid_state, norm_gain, conv_weight, filter_weight, degree_keep):
    hp = lax.Precision.HIGHEST
    float_type = grid_state.dtype
    channels = grid_state.shape[2]
    for depth_index in range(2):
        scale_rows = lax.rsqrt(lax.optimization_barrier(jnp.mean(grid_state * grid_state, axis=-1, keepdims=True)) + epsilon)
        normed = (grid_state * scale_rows * norm_gain[depth_index]).astype(jnp.bfloat16)
        wrapped = jnp.concatenate([normed[:, -1:], normed, normed[:, :1]], axis=1)
        padded = jnp.pad(wrapped, ((1, 1), (0, 0), (0, 0)))
        running = jnp.zeros((NLAT * NLON, channels), jnp.float32)
        for row_tap in range(3):
            for col_tap in range(3):
                window = padded[row_tap:row_tap + NLAT, col_tap:col_tap + NLON].reshape(NLAT * NLON, channels)
                running = running + jnp.dot(window, conv_weight[depth_index, row_tap, col_tap], preferred_element_type=jnp.float32)
        grid_state = grid_state + jax.nn.gelu(running.reshape(NLAT, NLON, channels).astype(float_type), approximate=False)
    rounded = lax.optimization_barrier(grid_state.astype(jnp.bfloat16))
    dft_table = forward_table(jnp.arange(NLON), DEGREES, NLON, float_type)
    spectrum = jnp.einsum('alc,lk->akc', rounded.astype(float_type), dft_table, precision=hp).astype(jnp.bfloat16)
    cosine, sine_values = colatitude(jnp.arange(NLAT), NLAT, float_type)
    assoc_basis = legendre_table(jnp.arange(DEGREES), cosine, sine_values, DEGREES)
    weighted = assoc_basis * (sine_values * (math.pi / NLAT))[None, None, :]
    values = lax.optimization_barrier(spectrum).astype(float_type).reshape(NLAT, DEGREES, 2, channels)
    coefficients = jnp.einsum('lmi,impc->lmpc', weighted, values, precision=hp).reshape(DEGREES, 2 * DEGREES, channels).astype(jnp.bfloat16)
    coefficients = lax.optimization_barrier(coefficients)
    mixing = jnp.einsum('lkc,lcd->lkd', coefficients.astype(float_type), filter_weight.astype(float_type), precision=hp)
    keep_mask = degree_keep.astype(float_type)
    filtered = (mixing.reshape(DEGREES, DEGREES, 2, channels) * keep_mask[:, :, None, None]).astype(jnp.bfloat16)
    filtered = lax.optimization_barrier(filtered)
    synthesis = jnp.einsum('lmi,lmpc->impc', assoc_basis, filtered.astype(float_type), precision=hp).reshape(NLAT, 2 * DEGREES, channels).astype(jnp.bfloat16)
    synthesis = lax.optimization_barrier(synthesis)
    physical = jnp.einsum('akc,kl->alc', synthesis.astype(float_type), inverse_table(DEGREES, NLON, float_type), precision=hp).astype(jnp.bfloat16)
    physical = lax.optimization_barrier(physical)
    return grid_state + jax.nn.gelu(physical.astype(float_type), approximate=False)
```

```python
import functools
import math

import jax
import jax.numpy as jnp
import ml_dtypes
import numpy as np
from jax import lax
from jax.experimental import pallas as pl
from jax.experimental.pallas import tpu as pltpu
from jax.sharding import PartitionSpec as P

epsilon = 1e-06
LANES = 128
MESH = pl.DeviceIdType.MESH
f32 = jnp.float32
bf16 = jnp.bfloat16


def up(value, step):
    return -(-value // step) * step


def gelu(value):
    return 0.5 * value * (1.0 + lax.erf(value * math.sqrt(0.5)))


def split(table):
    upper = table.astype(ml_dtypes.bfloat16)
    lower = (table - upper.astype(np.float64)).astype(ml_dtypes.bfloat16)
    return np.stack([upper, lower])


def fourier_tables(lon_parts, cols, col_pad, orders, mode_pad):
    total = lon_parts * cols
    forward = np.zeros((lon_parts, mode_pad, lon_parts, col_pad))
    inverse = np.zeros((lon_parts, col_pad, lon_parts, mode_pad))
    m = np.arange(lon_parts * orders)[:, None]
    j = np.arange(total)[None, :]
    phase = (m * j % total) * (2.0 * math.pi / total)
    pair = np.stack([np.cos(phase), -np.sin(phase)], axis=1)
    pair = pair.reshape(lon_parts, 2 * orders, lon_parts, cols)
    weight = np.where(m == 0, 1.0, 2.0)[:, :, None]
    back = (np.stack([np.cos(phase), -np.sin(phase)], axis=1) * weight).reshape(pair.shape)
    forward[:, : 2 * orders, :, :cols] = pair * (2.0 * math.pi / total)
    inverse[:, :cols, :, : 2 * orders] = back.transpose(2, 3, 0, 1)
    side_m, side_c = lon_parts * mode_pad, lon_parts * col_pad
    return split(forward.reshape(side_m, side_c)), split(inverse.reshape(side_c, side_m))


def legendre_seeds(lon_parts, orders, mode_pad, degrees, rows):
    count = lon_parts * orders
    m = np.arange(count, dtype=np.float64)[:, None]
    l = np.arange(degrees, dtype=np.float64)[None, :]
    theta = (np.arange(rows) + 0.5) * (math.pi / rows)
    gammas = np.array([math.lgamma(v + 0.5) - math.lgamma(v + 1.0) for v in range(count)])
    log_start = 0.5 * (
        np.log((2.0 * m + 1.0) / (4.0 * math.pi)) + gammas[:, None] - 0.5 * math.log(math.pi)
    ) + m * np.log(np.sin(theta))[None, :]
    growth = np.where(
        l > m, np.sqrt(np.maximum(4 * l * l - 1, 1) / np.maximum(l * l - m * m, 1)), 0.0
    )
    prior = l - 1.0
    damping = np.sqrt(
        np.maximum(prior * prior - m * m, 0) / np.maximum(4 * prior * prior - 1, 1)
    )
    table = np.concatenate([growth, damping, (l == m) * 1.0, np.exp(log_start)], axis=1)
    table = np.repeat(table.reshape(lon_parts, orders, -1), 2, axis=1)
    full = np.zeros((lon_parts, mode_pad, table.shape[2]), np.float32)
    full[:, : 2 * orders] = table
    lines = np.stack([np.cos(theta), np.sin(theta) * (math.pi / rows)]).astype(np.float32)
    return full, np.concatenate([lines, np.zeros((6, rows), np.float32)])


def conv_kernel(
    lat_parts, lon_parts, chunk,
    x_ref, gain_ref, w_hbm, out_ref, flat_ref,
    state, taps, weights, col_send, col_recv, row_recv, corners,
    w_sem, send_sem, recv_sem,
):
    rows, cols, channels = x_ref.shape
    pad = state.shape[1]
    col_rows = col_send.shape[2]
    lat, lon = lax.axis_index("lat"), lax.axis_index("lon")
    loads = [
        pltpu.make_async_copy(w_hbm.at[k], weights.at[k], w_sem.at[k]) for k in range(2)
    ]
    for load in loads:
        load.start()
    north = lax.rem(lat + lat_parts - 1, lat_parts)
    south = lax.rem(lat + 1, lat_parts)
    west = lax.rem(lon + lon_parts - 1, lon_parts)
    east = lax.rem(lon + 1, lon_parts)
    around = [
        (north, lon), (south, lon), (lat, west), (lat, east),
        (north, west), (south, west), (north, east), (south, east),
    ]
    barrier = pltpu.get_barrier_semaphore()
    for device in around:
        pl.semaphore_signal(barrier, inc=1, device_id=device, device_id_type=MESH)
    spot = lax.broadcasted_iota(jnp.int32, (pad, channels), 0)
    for r in range(rows):
        state[r, pl.ds(cols, pad - cols), :] = jnp.zeros((pad - cols, channels), f32)
        state[r, pl.ds(0, cols), :] = x_ref[r]
    col_send[...] = jnp.zeros(col_send.shape, f32)

    for k in range(2):
        gain = gain_ref[k : k + 1, :]
        for r in range(rows):
            value = state[r]
            scale = lax.rsqrt(jnp.mean(value * value, axis=-1, keepdims=True) + epsilon)
            normed = (value * scale * gain).astype(bf16)
            taps[k, 1, pl.ds((r + 1) * pad, pad), :] = normed
            wide = normed.astype(f32)
            col_send[k, 0, pl.ds(r, 1), :] = wide[0:1]
            col_send[k, 1, pl.ds(r, 1), :] = wide[cols - 1 : cols]
        if k == 0:
            pl.semaphore_wait(barrier, 8)
        routes = [
            (taps.at[k, 1, pl.ds(pad, pad)], row_recv.at[k, 1]),
            (taps.at[k, 1, pl.ds(rows * pad, pad)], row_recv.at[k, 0]),
            (col_send.at[k, 0], col_recv.at[k, 1]),
            (col_send.at[k, 1], col_recv.at[k, 0]),
            (col_send.at[k, 0, pl.ds(0, 8)], corners.at[k, 0]),
            (col_send.at[k, 0, pl.ds(col_rows - 8, 8)], corners.at[k, 1]),
            (col_send.at[k, 1, pl.ds(0, 8)], corners.at[k, 2]),
            (col_send.at[k, 1, pl.ds(col_rows - 8, 8)], corners.at[k, 3]),
        ]
        copies = []
        for n, (source, target) in enumerate(routes):
            copies.append(
                pltpu.make_async_remote_copy(
                    src_ref=source, dst_ref=target,
                    send_sem=send_sem.at[k, n], recv_sem=recv_sem.at[k, n],
                    device_id=around[n], device_id_type=MESH,
                )
            )
            copies[-1].start()
        loads[k].wait()
        for copy in copies:
            copy.wait()

        def place(line, wide, before, after):
            at = pl.ds(line * pad, pad)
            left = jnp.where(spot == 0, before, pltpu.roll(wide, 1, 0))
            right = jnp.where(spot == cols - 1, after, pltpu.roll(wide, pad - 1, 0))
            taps[k, 0, at, :] = left.astype(bf16)
            taps[k, 2, at, :] = right.astype(bf16)

        for r in range(rows):
            place(
                r + 1, taps[k, 1, pl.ds((r + 1) * pad, pad), :].astype(f32),
                col_recv[k, 0, pl.ds(r, 1), :], col_recv[k, 1, pl.ds(r, 1), :],
            )
        low = rows - 1 - (col_rows - 8)
        for side, line, inside, west_at, east_at, row in (
            (0, 0, lat > 0, 3, 1, low),
            (1, rows + 1, lat < lat_parts - 1, 2, 0, 0),
        ):
            wide = jnp.where(inside, row_recv[k, side].astype(f32), 0.0)
            taps[k, 1, pl.ds(line * pad, pad), :] = wide.astype(bf16)
            place(
                line, wide,
                jnp.where(inside, corners[k, west_at, pl.ds(row, 1), :], 0.0),
                jnp.where(inside, corners[k, east_at, pl.ds(row, 1), :], 0.0),
            )
        total = jnp.zeros((rows * pad, channels), f32)
        for a in range(3):
            for b in range(3):
                total = total + jnp.dot(
                    taps[k, b, pl.ds(a * pad, rows * pad), :], weights[k, a, b],
                    preferred_element_type=f32,
                )
        fresh = state[...].reshape(rows * pad, channels) + gelu(total)
        if k == 0:
            state[...] = fresh.reshape(rows, pad, channels)
        else:
            for r in range(rows):
                piece = fresh[r * pad : (r + 1) * pad]
                out_ref[r] = piece[:cols]
                flat_ref[:, pl.ds(r * channels, channels)] = jnp.where(
                    spot < cols, piece, 0.0
                ).astype(bf16)
    tail = flat_ref.shape[1] - rows * channels
    if tail:
        flat_ref[:, pl.ds(rows * channels, tail)] = jnp.zeros((pad, tail), bf16)


def spectral_kernel(
    lat_parts, lon_parts, chunk, mode_pad,
    flat_ref, x_ref, keep_ref, fwd_ref, inv_ref, seed_ref, line_ref, fw_hbm, out_ref,
    columns, spec_out, spec_in, lat_spec, lat_filt, syn_out, syn_in, phys_out, phys_in,
    basis, fw, fw_sem, lon_send, lon_recv, lat_send, lat_recv,
):
    rows, cols, channels = x_ref.shape
    pad = flat_ref.shape[0]
    degrees = fw.shape[0]
    total_rows = rows * lat_parts
    total_degrees = degrees * lat_parts
    tiles = channels // LANES
    per = chunk // LANES
    lat, lon = lax.axis_index("lat"), lax.axis_index("lon")
    load = pltpu.make_async_copy(fw_hbm, fw, fw_sem)
    load.start()
    barrier = pltpu.get_barrier_semaphore()
    lon_peers = [lax.rem(lon + s, lon_parts) for s in range(1, lon_parts)]
    lat_peers = [lax.rem(lat + s, lat_parts) for s in range(1, lat_parts)]
    for peer in lon_peers:
        pl.semaphore_signal(barrier, inc=1, device_id=(lat, peer), device_id_type=MESH)
    for peer in lat_peers:
        pl.semaphore_signal(barrier, inc=1, device_id=(peer, lon), device_id_type=MESH)
    pl.semaphore_wait(barrier, lon_parts + lat_parts - 2)

    def scatter(phase, source_of, target):
        copies = []
        for s, peer in enumerate(lon_peers):
            copies.append(
                pltpu.make_async_remote_copy(
                    src_ref=source_of(peer), dst_ref=target.at[lon],
                    send_sem=lon_send.at[phase, s], recv_sem=lon_recv.at[phase, s],
                    device_id=(lat, peer), device_id_type=MESH,
                )
            )
            copies[-1].start()
        return copies

    def spread(phase, buffer):
        copies = []
        for s, peer in enumerate(lat_peers):
            copies.append(
                pltpu.make_async_remote_copy(
                    src_ref=buffer.at[lat], dst_ref=buffer.at[lat],
                    send_sem=lat_send.at[phase, s], recv_sem=lat_recv.at[phase, s],
                    device_id=(peer, lon), device_id_type=MESH,
                )
            )
            copies[-1].start()
        return copies

    def finish(copies):
        for copy in copies:
            copy.wait()

    def lane_block(part):
        return pl.ds(pl.multiple_of(part * chunk, LANES), chunk)

    def both(table, data):
        first = jnp.dot(table[0], data, preferred_element_type=f32)
        return first + jnp.dot(table[1], data, preferred_element_type=f32)

    copies = scatter(0, lambda peer: flat_ref.at[:, lane_block(peer)], columns)
    columns[lon] = flat_ref[:, lane_block(lon)]

    seeds = seed_ref[lon]
    growth = seeds[:, :total_degrees]
    damping = seeds[:, total_degrees : 2 * total_degrees]
    start = seeds[:, 2 * total_degrees : 3 * total_degrees]
    sectoral = seeds[:, 3 * total_degrees :]
    cosine = line_ref[0:1, :]
    before = jnp.zeros((mode_pad, total_rows), f32)
    latest = before
    for l in range(total_degrees):
        grown = growth[:, l : l + 1] * (cosine * latest - damping[:, l : l + 1] * before)
        before, latest = latest, grown + start[:, l : l + 1] * sectoral
        basis[pl.ds(l * mode_pad, mode_pad), :] = latest

    def expand(values, first_row, lines):
        wide = lines * mode_pad
        row = lax.broadcasted_iota(jnp.int32, (total_rows, wide), 0)
        column = lax.broadcasted_iota(jnp.int32, (total_rows, wide), 1)
        low = row * mode_pad
        at = column + first_row * mode_pad
        pick = jnp.where((at >= low) & (at < low + mode_pad), 1.0, 0.0).astype(bf16)
        upper = values.astype(bf16)
        lower = (values - upper.astype(f32)).astype(bf16)
        shape = (values.shape[0], wide)
        own = lax.rem(lax.broadcasted_iota(jnp.int32, shape, 0), mode_pad)
        other = lax.rem(lax.broadcasted_iota(jnp.int32, shape, 1), mode_pad)
        same = own == other
        return [
            jnp.where(same, jnp.dot(part, pick, preferred_element_type=f32), 0.0).astype(bf16)
            for part in (upper, lower)
        ]

    own_rows = pl.ds(pl.multiple_of(lat * degrees * mode_pad, 16), degrees * mode_pad)
    analysis = expand(basis[own_rows, :] * line_ref[1:2, :], 0, total_rows)
    rebuild = expand(basis[...], lat * rows, rows)

    finish(copies)
    spectrum = both(fwd_ref, columns[...].reshape(lon_parts * pad, chunk))
    spec_out[...] = spectrum.astype(bf16).reshape(spec_out.shape)
    copies = scatter(1, lambda peer: spec_out.at[peer], spec_in)
    spec_in[lon] = spec_out[lon]
    finish(copies)
    for i in range(rows):
        for c in range(tiles):
            part, tile = divmod(i * tiles + c, per)
            lat_spec[lat, pl.ds(i * mode_pad, mode_pad), pl.ds(c * LANES, LANES)] = spec_in[
                part, :, pl.ds(tile * LANES, LANES)
            ]
    finish(spread(0, lat_spec))
    coefficients = both(
        analysis, lat_spec[...].reshape(total_rows * mode_pad, channels)
    ).astype(bf16)
    load.wait()
    for l in range(degrees):
        at = pl.ds(l * mode_pad, mode_pad)
        mixed = jnp.dot(
            coefficients[l * mode_pad : (l + 1) * mode_pad], fw[l], preferred_element_type=f32
        )
        lat_filt[lat, at, :] = (mixed * keep_ref[at, :]).astype(bf16)
    finish(spread(1, lat_filt))
    filtered = lat_filt[...].reshape(total_degrees * mode_pad, channels)
    over = (((0,), (0,)), ((), ()))
    synthesis = sum(
        lax.dot_general(part, filtered, over, preferred_element_type=f32) for part in rebuild
    ).astype(bf16)
    syn_out[...] = jnp.zeros(syn_out.shape, bf16)
    for i in range(rows):
        for c in range(tiles):
            part, tile = divmod(i * tiles + c, per)
            syn_out[part, :, pl.ds(tile * LANES, LANES)] = synthesis[
                i * mode_pad : (i + 1) * mode_pad, c * LANES : (c + 1) * LANES
            ]
    copies = scatter(2, lambda peer: syn_out.at[peer], syn_in)
    syn_in[lon] = syn_out[lon]
    finish(copies)
    physical = both(inv_ref, syn_in[...].reshape(lon_parts * mode_pad, chunk))
    phys_out[...] = physical.astype(bf16).reshape(phys_out.shape)
    copies = scatter(3, lambda peer: phys_out.at[peer], phys_in)
    phys_in[lon] = phys_out[lon]
    finish(copies)
    for i in range(rows):
        for c in range(tiles):
            part, tile = divmod(i * tiles + c, per)
            at = pl.ds(c * LANES, LANES)
            value = phys_in[part, :, pl.ds(tile * LANES, LANES)].astype(f32)
            out_ref[i, :, at] = x_ref[i, :, at] + gelu(value)[:cols]


def per_device(grid_state, norm_gain, conv_weight, filter_weight, degree_keep):
    rows, cols, channels = grid_state.shape
    lat_parts, lon_parts = lax.axis_size("lat"), lax.axis_size("lon")
    degrees, orders = degree_keep.shape
    col_pad, mode_pad = up(cols, 16), up(2 * orders, 16)
    col_rows = up(rows, 8)
    chunk = up(-(-rows * channels // lon_parts), LANES)
    vmem = pl.BlockSpec(memory_space=pltpu.VMEM)
    hbm = pl.BlockSpec(memory_space=pl.ANY)
    dma = pltpu.SemaphoreType.DMA
    x, flat = pl.pallas_call(
        functools.partial(conv_kernel, lat_parts, lon_parts, chunk),
        out_shape=(
            jax.ShapeDtypeStruct((rows, cols, channels), f32),
            jax.ShapeDtypeStruct((col_pad, lon_parts * chunk), bf16),
        ),
        in_specs=[vmem, vmem, hbm],
        out_specs=(vmem, vmem),
        scratch_shapes=[
            pltpu.VMEM((rows, col_pad, channels), f32),
            pltpu.VMEM((2, 3, (rows + 2) * col_pad, channels), bf16),
            pltpu.VMEM((2, 3, 3, channels, channels), bf16),
            pltpu.VMEM((2, 2, col_rows, channels), f32),
            pltpu.VMEM((2, 2, col_rows, channels), f32),
            pltpu.VMEM((2, 2, col_pad, channels), bf16),
            pltpu.VMEM((2, 4, 8, channels), f32),
            dma((2,)),
            dma((2, 8)),
            dma((2, 8)),
        ],
        compiler_params=pltpu.CompilerParams(collective_id=0, has_side_effects=True),
        name="conv_pair",
    )(grid_state, norm_gain, conv_weight)

    forward, inverse = fourier_tables(lon_parts, cols, col_pad, orders, mode_pad)
    seeds, lines = legendre_seeds(
        lon_parts, orders, mode_pad, degrees * lat_parts, rows * lat_parts
    )
    keep = jnp.repeat(degree_keep.astype(f32), 2, axis=1)
    keep = jnp.pad(keep, ((0, 0), (0, mode_pad - 2 * orders))).reshape(degrees * mode_pad, 1)
    block = pltpu.VMEM((lon_parts, mode_pad, chunk), bf16)
    column_block = pltpu.VMEM((lon_parts, col_pad, chunk), bf16)
    return pl.pallas_call(
        functools.partial(spectral_kernel, lat_parts, lon_parts, chunk, mode_pad),
        out_shape=jax.ShapeDtypeStruct((rows, cols, channels), f32),
        in_specs=[vmem] * 7 + [hbm],
        out_specs=vmem,
        scratch_shapes=[
            column_block,
            block,
            block,
            pltpu.VMEM((lat_parts, rows * mode_pad, channels), bf16),
            pltpu.VMEM((lat_parts, degrees * mode_pad, channels), bf16),
            block,
            block,
            column_block,
            column_block,
            pltpu.VMEM((degrees * lat_parts * mode_pad, rows * lat_parts), f32),
            pltpu.VMEM((degrees, channels, channels), bf16),
            dma(()),
            dma((4, lon_parts - 1)),
            dma((4, lon_parts - 1)),
            dma((2, lat_parts - 1)),
            dma((2, lat_parts - 1)),
        ],
        compiler_params=pltpu.CompilerParams(collective_id=1, has_side_effects=True),
        name="spectral_block",
    )(
        flat, x, keep, jnp.asarray(forward), jnp.asarray(inverse),
        jnp.asarray(seeds), jnp.asarray(lines), filter_weight,
    )


def solution(mesh):
    in_specs = (P("lat", "lon", None), P(), P(), P("lat", None, None), P("lat", "lon"))
    out_specs = P("lat", "lon", None)
    return jax.shard_map(
        per_device, mesh=mesh, in_specs=in_specs, out_specs=out_specs, check_vma=False
    )
```

```python
import functools
import math

import jax
import jax.numpy as jnp
import ml_dtypes
import numpy as np
from jax import lax
from jax.experimental import pallas as pl
from jax.experimental.pallas import tpu as pltpu
from jax.sharding import PartitionSpec as P

epsilon = 1e-06
LANES = 128
MESH = pl.DeviceIdType.MESH
f32 = jnp.float32
bf16 = jnp.bfloat16


def up(value, step):
    return -(-value // step) * step


def gelu(value):
    return 0.5 * value * (1.0 + lax.erf(value * math.sqrt(0.5)))


def split(table):
    upper = table.astype(ml_dtypes.bfloat16)
    lower = (table - upper.astype(np.float64)).astype(ml_dtypes.bfloat16)
    return np.stack([upper, lower])


def fourier_tables(lon_parts, cols, col_pad, orders, mode_pad):
    total = lon_parts * cols
    forward = np.zeros((lon_parts, mode_pad, lon_parts, col_pad))
    inverse = np.zeros((lon_parts, col_pad, lon_parts, mode_pad))
    m = np.arange(lon_parts * orders)[:, None]
    j = np.arange(total)[None, :]
    phase = (m * j % total) * (2.0 * math.pi / total)
    pair = np.stack([np.cos(phase), -np.sin(phase)], axis=1)
    pair = pair.reshape(lon_parts, 2 * orders, lon_parts, cols)
    weight = np.where(m == 0, 1.0, 2.0)[:, :, None]
    back = (np.stack([np.cos(phase), -np.sin(phase)], axis=1) * weight).reshape(pair.shape)
    forward[:, : 2 * orders, :, :cols] = pair * (2.0 * math.pi / total)
    inverse[:, :cols, :, : 2 * orders] = back.transpose(2, 3, 0, 1)
    side_m, side_c = lon_parts * mode_pad, lon_parts * col_pad
    return split(forward.reshape(side_m, side_c)), split(inverse.reshape(side_c, side_m))


def legendre_seeds(lon_parts, orders, mode_pad, degrees, rows):
    count = lon_parts * orders
    m = np.arange(count, dtype=np.float64)[:, None]
    l = np.arange(degrees, dtype=np.float64)[None, :]
    theta = (np.arange(rows) + 0.5) * (math.pi / rows)
    gammas = np.array([math.lgamma(v + 0.5) - math.lgamma(v + 1.0) for v in range(count)])
    log_start = 0.5 * (
        np.log((2.0 * m + 1.0) / (4.0 * math.pi)) + gammas[:, None] - 0.5 * math.log(math.pi)
    ) + m * np.log(np.sin(theta))[None, :]
    growth = np.where(
        l > m, np.sqrt(np.maximum(4 * l * l - 1, 1) / np.maximum(l * l - m * m, 1)), 0.0
    )
    prior = l - 1.0
    damping = np.sqrt(
        np.maximum(prior * prior - m * m, 0) / np.maximum(4 * prior * prior - 1, 1)
    )
    table = np.concatenate([growth, damping, (l == m) * 1.0, np.exp(log_start)], axis=1)
    table = np.repeat(table.reshape(lon_parts, orders, -1), 2, axis=1)
    full = np.zeros((lon_parts, up(mode_pad, 8), table.shape[2]), np.float32)
    full[:, : 2 * orders] = table
    lines = np.stack([np.cos(theta), np.sin(theta) * (math.pi / rows)]).astype(np.float32)
    return full, np.concatenate([lines, np.zeros((6, rows), np.float32)])


def block_kernel(
    lat_parts, lon_parts, chunk, modes,
    x_ref, gain_ref, keep_ref, fwd_ref, inv_ref, seed_ref, line_ref, w_hbm, fw_hbm, out_ref,
    state, taps, weights, col_send, col_recv, row_recv, corners, flat,
    columns, spec_out, spec_in, lat_spec, lat_filt, syn_out, syn_in, phys_out, phys_in,
    basis, analysis, rebuild, packed, fw,
    w_sem, fw_sem, send_sem, recv_sem, lon_send, lon_recv, lat_send, lat_recv,
):
    rows, cols, channels = x_ref.shape
    pad = state.shape[1]
    mode_pad = spec_in.shape[1]
    col_rows = col_send.shape[2]
    degrees = fw.shape[0]
    total_rows = rows * lat_parts
    total_degrees = degrees * lat_parts
    tiles = channels // LANES
    per = chunk // LANES
    lat, lon = lax.axis_index("lat"), lax.axis_index("lon")
    loads = [
        pltpu.make_async_copy(w_hbm.at[k], weights.at[k], w_sem.at[k]) for k in range(2)
    ]
    loads.append(pltpu.make_async_copy(fw_hbm, fw, fw_sem))
    for load in loads:
        load.start()
    north = lax.rem(lat + lat_parts - 1, lat_parts)
    south = lax.rem(lat + 1, lat_parts)
    west = lax.rem(lon + lon_parts - 1, lon_parts)
    east = lax.rem(lon + 1, lon_parts)
    lon_peers = [lax.rem(lon + s, lon_parts) for s in range(1, lon_parts)]
    lat_peers = [lax.rem(lat + s, lat_parts) for s in range(1, lat_parts)]
    corner_peers = [(north, west), (south, west), (north, east), (south, east)]
    around = [(north, lon), (south, lon), (lat, west), (lat, east)] + corner_peers
    greeted = [(lat, peer) for peer in lon_peers] + [(peer, lon) for peer in lat_peers]
    greeted += corner_peers
    barrier = pltpu.get_barrier_semaphore()
    for device in greeted:
        pl.semaphore_signal(barrier, inc=1, device_id=device, device_id_type=MESH)
    spot = lax.broadcasted_iota(jnp.int32, (pad, channels), 0)
    for r in range(rows):
        state[r, pl.ds(cols, pad - cols), :] = jnp.zeros((pad - cols, channels), f32)
        state[r, pl.ds(0, cols), :] = x_ref[r]
    col_send[...] = jnp.zeros(col_send.shape, f32)

    def legendre():
        seeds = seed_ref[lon]
        growth = seeds[:, :total_degrees]
        damping = seeds[:, total_degrees : 2 * total_degrees]
        start = seeds[:, 2 * total_degrees : 3 * total_degrees]
        sectoral = seeds[:, 3 * total_degrees :]
        cosine = line_ref[0:1, :]
        before = jnp.zeros(sectoral.shape, f32)
        latest = before
        for l in range(total_degrees):
            grown = growth[:, l : l + 1] * (cosine * latest - damping[:, l : l + 1] * before)
            before, latest = latest, grown + start[:, l : l + 1] * sectoral
            basis[pl.ds(l * modes, modes), :] = latest[:modes]

    def expand(values, first_row, target):
        shape = target.shape[1:]
        row = lax.broadcasted_iota(jnp.int32, (total_rows, shape[1]), 0) * modes
        at = lax.broadcasted_iota(jnp.int32, (total_rows, shape[1]), 1) + first_row * modes
        pick = jnp.where((at >= row) & (at < row + modes), 1.0, 0.0).astype(bf16)
        upper = values.astype(bf16)
        lower = (values - upper.astype(f32)).astype(bf16)
        own = lax.rem(lax.broadcasted_iota(jnp.int32, shape, 0), modes)
        other = lax.rem(lax.broadcasted_iota(jnp.int32, shape, 1), modes)
        same = own == other
        for n, part in enumerate((upper, lower)):
            wide = jnp.dot(part, pick, preferred_element_type=f32)
            target[n] = jnp.where(same, wide, 0.0).astype(bf16)

    def place(k, line, wide, before, after):
        at = pl.ds(line * pad, pad)
        left = jnp.where(spot == 0, before, pltpu.roll(wide, 1, 0))
        right = jnp.where(spot == cols - 1, after, pltpu.roll(wide, pad - 1, 0))
        taps[k, 0, at, :] = left.astype(bf16)
        taps[k, 2, at, :] = right.astype(bf16)

    for k in range(2):
        gain = gain_ref[k : k + 1, :]
        for r in range(rows):
            value = state[r]
            scale = lax.rsqrt(jnp.mean(value * value, axis=-1, keepdims=True) + epsilon)
            normed = (value * scale * gain).astype(bf16)
            taps[k, 1, pl.ds((r + 1) * pad, pad), :] = normed
            wide = normed.astype(f32)
            col_send[k, 0, pl.ds(r, 1), :] = wide[0:1]
            col_send[k, 1, pl.ds(r, 1), :] = wide[cols - 1 : cols]
        if k == 0:
            pl.semaphore_wait(barrier, len(greeted))
        routes = [
            (taps.at[k, 1, pl.ds(pad, pad)], row_recv.at[k, 1]),
            (taps.at[k, 1, pl.ds(rows * pad, pad)], row_recv.at[k, 0]),
            (col_send.at[k, 0], col_recv.at[k, 1]),
            (col_send.at[k, 1], col_recv.at[k, 0]),
            (col_send.at[k, 0, pl.ds(0, 8)], corners.at[k, 0]),
            (col_send.at[k, 0, pl.ds(col_rows - 8, 8)], corners.at[k, 1]),
            (col_send.at[k, 1, pl.ds(0, 8)], corners.at[k, 2]),
            (col_send.at[k, 1, pl.ds(col_rows - 8, 8)], corners.at[k, 3]),
        ]
        copies = []
        for n, (source, target) in enumerate(routes):
            copies.append(
                pltpu.make_async_remote_copy(
                    src_ref=source, dst_ref=target,
                    send_sem=send_sem.at[k, n], recv_sem=recv_sem.at[k, n],
                    device_id=around[n], device_id_type=MESH,
                )
            )
        for n in (4, 5, 6, 7, 0, 1, 2, 3):
            copies[n].start()
        if k == 0:
            legendre()
            own_rows = pl.ds(pl.multiple_of(lat * degrees * modes, 8), degrees * modes)
            expand(basis[own_rows, :] * line_ref[1:2, :], 0, analysis)
        else:
            expand(basis[...], lat * rows, rebuild)
        loads[k].wait()
        for copy in copies:
            copy.wait()
        for r in range(rows):
            place(
                k, r + 1, taps[k, 1, pl.ds((r + 1) * pad, pad), :].astype(f32),
                col_recv[k, 0, pl.ds(r, 1), :], col_recv[k, 1, pl.ds(r, 1), :],
            )
        low = rows - 1 - (col_rows - 8)
        for side, line, inside, west_at, east_at, row in (
            (0, 0, lat > 0, 3, 1, low),
            (1, rows + 1, lat < lat_parts - 1, 2, 0, 0),
        ):
            wide = jnp.where(inside, row_recv[k, side].astype(f32), 0.0)
            taps[k, 1, pl.ds(line * pad, pad), :] = wide.astype(bf16)
            place(
                k, line, wide,
                jnp.where(inside, corners[k, west_at, pl.ds(row, 1), :], 0.0),
                jnp.where(inside, corners[k, east_at, pl.ds(row, 1), :], 0.0),
            )
        total = jnp.zeros((rows * pad, channels), f32)
        for a in range(3):
            for b in range(3):
                total = total + jnp.dot(
                    taps[k, b, pl.ds(a * pad, rows * pad), :], weights[k, a, b],
                    preferred_element_type=f32,
                )
        fresh = state[...].reshape(rows * pad, channels) + gelu(total)
        state[...] = fresh.reshape(rows, pad, channels)
    for r in range(rows):
        flat[:, pl.ds(r * channels, channels)] = jnp.where(
            spot < cols, state[r], 0.0
        ).astype(bf16)
    tail = flat.shape[1] - rows * channels
    if tail:
        flat[:, pl.ds(rows * channels, tail)] = jnp.zeros((pad, tail), bf16)

    def scatter(phase, source_of, target):
        copies = []
        for s, peer in enumerate(lon_peers):
            copies.append(
                pltpu.make_async_remote_copy(
                    src_ref=source_of(peer), dst_ref=target.at[lon],
                    send_sem=lon_send.at[phase, s], recv_sem=lon_recv.at[phase, s],
                    device_id=(lat, peer), device_id_type=MESH,
                )
            )
            copies[-1].start()
        return copies

    def spread(phase, buffer):
        copies = []
        for s, peer in enumerate(lat_peers):
            copies.append(
                pltpu.make_async_remote_copy(
                    src_ref=buffer.at[lat], dst_ref=buffer.at[lat],
                    send_sem=lat_send.at[phase, s], recv_sem=lat_recv.at[phase, s],
                    device_id=(peer, lon), device_id_type=MESH,
                )
            )
            copies[-1].start()
        return copies

    def finish(copies):
        for copy in copies:
            copy.wait()

    def lane_block(part):
        return pl.ds(pl.multiple_of(part * chunk, LANES), chunk)

    def both(table, data):
        first = jnp.dot(table[0], data, preferred_element_type=f32)
        return first + jnp.dot(table[1], data, preferred_element_type=f32)

    copies = scatter(0, lambda peer: flat.at[:, lane_block(peer)], columns)
    columns[lon] = flat[:, lane_block(lon)]
    finish(copies)
    spectrum = both(fwd_ref, columns[...].reshape(lon_parts * pad, chunk))
    spec_out[...] = spectrum.astype(bf16).reshape(spec_out.shape)
    copies = scatter(1, lambda peer: spec_out.at[peer], spec_in)
    spec_in[lon] = spec_out[lon]
    finish(copies)
    for i in range(rows):
        for c in range(tiles):
            part, tile = divmod(i * tiles + c, per)
            piece = spec_in[part, :, pl.ds(tile * LANES, LANES)].astype(f32)
            packed[pl.ds(i * modes, modes), pl.ds(c * LANES, LANES)] = piece[:modes]
    lat_spec[lat] = packed[pl.ds(0, rows * modes), :].astype(bf16)
    finish(spread(0, lat_spec))
    coefficients = both(analysis, lat_spec[...].reshape(total_rows * modes, channels))
    loads[2].wait()
    shape = (modes, keep_ref.shape[1])
    order = 2 * lax.broadcasted_iota(jnp.int32, shape, 1)
    mode = lax.broadcasted_iota(jnp.int32, shape, 0)
    mine = (mode >= order) & (mode < order + 2)
    for l in range(degrees):
        kept = jnp.where(mine, keep_ref[l : l + 1, :].astype(f32), 0.0)
        mixed = jnp.dot(
            coefficients[l * modes : (l + 1) * modes].astype(bf16), fw[l],
            preferred_element_type=f32,
        )
        packed[pl.ds(l * modes, modes), :] = mixed * jnp.sum(kept, axis=1, keepdims=True)
    lat_filt[lat] = packed[pl.ds(0, degrees * modes), :].astype(bf16)
    finish(spread(1, lat_filt))
    filtered = lat_filt[...].reshape(total_degrees * modes, channels)
    over = (((0,), (0,)), ((), ()))
    packed[pl.ds(0, rows * modes), :] = sum(
        lax.dot_general(rebuild[n], filtered, over, preferred_element_type=f32)
        for n in range(2)
    )
    packed[pl.ds(rows * modes, mode_pad), :] = jnp.zeros((mode_pad, channels), f32)
    syn_out[...] = jnp.zeros(syn_out.shape, bf16)
    for i in range(rows):
        for c in range(tiles):
            part, tile = divmod(i * tiles + c, per)
            syn_out[part, :, pl.ds(tile * LANES, LANES)] = packed[
                pl.ds(i * modes, mode_pad), pl.ds(c * LANES, LANES)
            ].astype(bf16)
    copies = scatter(2, lambda peer: syn_out.at[peer], syn_in)
    syn_in[lon] = syn_out[lon]
    finish(copies)
    physical = both(inv_ref, syn_in[...].reshape(lon_parts * mode_pad, chunk))
    phys_out[...] = physical.astype(bf16).reshape(phys_out.shape)
    copies = scatter(3, lambda peer: phys_out.at[peer], phys_in)
    phys_in[lon] = phys_out[lon]
    finish(copies)
    for i in range(rows):
        for c in range(tiles):
            part, tile = divmod(i * tiles + c, per)
            at = pl.ds(c * LANES, LANES)
            value = phys_in[part, :, pl.ds(tile * LANES, LANES)].astype(f32)
            out_ref[i, :, at] = (state[i, :, at] + gelu(value))[:cols]


def per_device(grid_state, norm_gain, conv_weight, filter_weight, degree_keep):
    rows, cols, channels = grid_state.shape
    lat_parts, lon_parts = lax.axis_size("lat"), lax.axis_size("lon")
    degrees, orders = degree_keep.shape
    modes = 2 * orders
    col_pad, mode_pad = up(cols, 16), up(modes, 16)
    col_rows = up(rows, 8)
    chunk = up(-(-rows * channels // lon_parts), LANES)
    total_rows, total_degrees = rows * lat_parts, degrees * lat_parts
    vmem = pl.BlockSpec(memory_space=pltpu.VMEM)
    hbm = pl.BlockSpec(memory_space=pl.ANY)
    dma = pltpu.SemaphoreType.DMA
    forward, inverse = fourier_tables(lon_parts, cols, col_pad, orders, mode_pad)
    seeds, lines = legendre_seeds(lon_parts, orders, modes, total_degrees, total_rows)
    block = pltpu.VMEM((lon_parts, mode_pad, chunk), bf16)
    column_block = pltpu.VMEM((lon_parts, col_pad, chunk), bf16)
    return pl.pallas_call(
        functools.partial(block_kernel, lat_parts, lon_parts, chunk, modes),
        out_shape=jax.ShapeDtypeStruct((rows, cols, channels), f32),
        in_specs=[vmem] * 7 + [hbm, hbm],
        out_specs=vmem,
        scratch_shapes=[
            pltpu.VMEM((rows, col_pad, channels), f32),
            pltpu.VMEM((2, 3, (rows + 2) * col_pad, channels), bf16),
            pltpu.VMEM((2, 3, 3, channels, channels), bf16),
            pltpu.VMEM((2, 2, col_rows, channels), f32),
            pltpu.VMEM((2, 2, col_rows, channels), f32),
            pltpu.VMEM((2, 2, col_pad, channels), bf16),
            pltpu.VMEM((2, 4, 8, channels), f32),
            pltpu.VMEM((col_pad, lon_parts * chunk), bf16),
            column_block,
            block,
            block,
            pltpu.VMEM((lat_parts, rows * modes, channels), bf16),
            pltpu.VMEM((lat_parts, degrees * modes, channels), bf16),
            block,
            block,
            column_block,
            column_block,
            pltpu.VMEM((total_degrees * modes, total_rows), f32),
            pltpu.VMEM((2, degrees * modes, total_rows * modes), bf16),
            pltpu.VMEM((2, total_degrees * modes, rows * modes), bf16),
            pltpu.VMEM((max(rows, degrees) * modes + mode_pad, channels), f32),
            pltpu.VMEM((degrees, channels, channels), bf16),
            dma((2,)),
            dma(()),
            dma((2, 8)),
            dma((2, 8)),
            dma((4, lon_parts - 1)),
            dma((4, lon_parts - 1)),
            dma((2, lat_parts - 1)),
            dma((2, lat_parts - 1)),
        ],
        compiler_params=pltpu.CompilerParams(collective_id=0, has_side_effects=True),
        name="block",
    )(
        grid_state, norm_gain, degree_keep, jnp.asarray(forward), jnp.asarray(inverse),
        jnp.asarray(seeds), jnp.asarray(lines), conv_weight, filter_weight,
    )


def solution(mesh):
    in_specs = (P("lat", "lon", None), P(), P(), P("lat", None, None), P("lat", "lon"))
    out_specs = P("lat", "lon", None)
    return jax.shard_map(
        per_device, mesh=mesh, in_specs=in_specs, out_specs=out_specs, check_vma=False
    )
```

```python
import functools
import math

import jax
import jax.numpy as jnp
import ml_dtypes
import numpy as np
from jax import lax
from jax.experimental import pallas as pl
from jax.experimental.pallas import tpu as pltpu
from jax.sharding import PartitionSpec as P

epsilon = 1e-06
LANES = 128
MESH = pl.DeviceIdType.MESH
f32 = jnp.float32
bf16 = jnp.bfloat16


def up(value, step):
    return -(-value // step) * step


def gelu(value):
    return 0.5 * value * (1.0 + lax.erf(value * math.sqrt(0.5)))


def split(table):
    upper = table.astype(ml_dtypes.bfloat16)
    lower = (table - upper.astype(np.float64)).astype(ml_dtypes.bfloat16)
    return np.stack([upper, lower])


def fourier_tables(lon_parts, cols, col_pad, orders, mode_pad):
    total = lon_parts * cols
    forward = np.zeros((lon_parts, mode_pad, lon_parts, col_pad))
    inverse = np.zeros((lon_parts, col_pad, lon_parts, mode_pad))
    m = np.arange(lon_parts * orders)[:, None]
    j = np.arange(total)[None, :]
    phase = (m * j % total) * (2.0 * math.pi / total)
    pair = np.stack([np.cos(phase), -np.sin(phase)], axis=1)
    pair = pair.reshape(lon_parts, 2 * orders, lon_parts, cols)
    weight = np.where(m == 0, 1.0, 2.0)[:, :, None]
    back = (np.stack([np.cos(phase), -np.sin(phase)], axis=1) * weight).reshape(pair.shape)
    forward[:, : 2 * orders, :, :cols] = pair * (2.0 * math.pi / total)
    inverse[:, :cols, :, : 2 * orders] = back.transpose(2, 3, 0, 1)
    side_m, side_c = lon_parts * mode_pad, lon_parts * col_pad
    return split(forward.reshape(side_m, side_c)), split(inverse.reshape(side_c, side_m))


def legendre_seeds(lon_parts, orders, mode_pad, degrees, rows):
    count = lon_parts * orders
    m = np.arange(count, dtype=np.float64)[:, None]
    l = np.arange(degrees, dtype=np.float64)[None, :]
    theta = (np.arange(rows) + 0.5) * (math.pi / rows)
    gammas = np.array([math.lgamma(v + 0.5) - math.lgamma(v + 1.0) for v in range(count)])
    log_start = 0.5 * (
        np.log((2.0 * m + 1.0) / (4.0 * math.pi)) + gammas[:, None] - 0.5 * math.log(math.pi)
    ) + m * np.log(np.sin(theta))[None, :]
    growth = np.where(
        l > m, np.sqrt(np.maximum(4 * l * l - 1, 1) / np.maximum(l * l - m * m, 1)), 0.0
    )
    prior = l - 1.0
    damping = np.sqrt(
        np.maximum(prior * prior - m * m, 0) / np.maximum(4 * prior * prior - 1, 1)
    )
    table = np.concatenate([growth, damping, (l == m) * 1.0, np.exp(log_start)], axis=1)
    table = np.repeat(table.reshape(lon_parts, orders, -1), 2, axis=1)
    full = np.zeros((lon_parts, up(mode_pad, 8), table.shape[2]), np.float32)
    full[:, : 2 * orders] = table
    lines = np.stack([np.cos(theta), np.sin(theta) * (math.pi / rows)]).astype(np.float32)
    return full, np.concatenate([lines, np.zeros((6, rows), np.float32)])


def block_kernel(
    lat_parts, lon_parts, groups, modes,
    x_ref, gain_ref, keep_ref, fwd_ref, inv_ref, seed_ref, line_ref, w_hbm, fw_hbm, out_ref,
    state, taps, weights, col_send, col_recv, row_recv, corners, flat,
    columns, spec_out, spec_in, lat_spec, lat_filt, syn_out, syn_in, phys_out, phys_in,
    basis, analysis, rebuild, packed, mixed, fw,
    w_sem, fw_sem, send_sem, recv_sem, lon_send, lon_recv, lat_send, lat_recv,
):
    rows, cols, channels = x_ref.shape
    pad = state.shape[1]
    mode_pad = spec_in[0].shape[1]
    col_rows = col_send.shape[2]
    degrees = fw.shape[0]
    total_rows = rows * lat_parts
    total_degrees = degrees * lat_parts
    lat, lon = lax.axis_index("lat"), lax.axis_index("lon")
    loads = [
        pltpu.make_async_copy(w_hbm.at[k], weights.at[k], w_sem.at[k]) for k in range(2)
    ]
    loads.append(pltpu.make_async_copy(fw_hbm, fw, fw_sem))
    for load in loads:
        load.start()
    north = lax.rem(lat + lat_parts - 1, lat_parts)
    south = lax.rem(lat + 1, lat_parts)
    west = lax.rem(lon + lon_parts - 1, lon_parts)
    east = lax.rem(lon + 1, lon_parts)
    lon_peers = [lax.rem(lon + s, lon_parts) for s in range(1, lon_parts)]
    lat_peers = [lax.rem(lat + s, lat_parts) for s in range(1, lat_parts)]
    corner_peers = [(north, west), (south, west), (north, east), (south, east)]
    around = [(north, lon), (south, lon), (lat, west), (lat, east)] + corner_peers
    greeted = [(lat, peer) for peer in lon_peers] + [(peer, lon) for peer in lat_peers]
    greeted += corner_peers
    barrier = pltpu.get_barrier_semaphore()
    for device in greeted:
        pl.semaphore_signal(barrier, inc=1, device_id=device, device_id_type=MESH)
    spot = lax.broadcasted_iota(jnp.int32, (pad, channels), 0)
    for r in range(rows):
        state[r, pl.ds(cols, pad - cols), :] = jnp.zeros((pad - cols, channels), f32)
        state[r, pl.ds(0, cols), :] = x_ref[r]
    col_send[...] = jnp.zeros(col_send.shape, f32)

    def legendre():
        seeds = seed_ref[lon]
        growth = seeds[:, :total_degrees]
        damping = seeds[:, total_degrees : 2 * total_degrees]
        start = seeds[:, 2 * total_degrees : 3 * total_degrees]
        sectoral = seeds[:, 3 * total_degrees :]
        cosine = line_ref[0:1, :]
        before = jnp.zeros(sectoral.shape, f32)
        latest = before
        for l in range(total_degrees):
            grown = growth[:, l : l + 1] * (cosine * latest - damping[:, l : l + 1] * before)
            before, latest = latest, grown + start[:, l : l + 1] * sectoral
            basis[pl.ds(l * modes, modes), :] = latest[:modes]

    def expand(values, first_row, target):
        shape = target.shape[1:]
        row = lax.broadcasted_iota(jnp.int32, (total_rows, shape[1]), 0) * modes
        at = lax.broadcasted_iota(jnp.int32, (total_rows, shape[1]), 1) + first_row * modes
        pick = jnp.where((at >= row) & (at < row + modes), 1.0, 0.0).astype(bf16)
        upper = values.astype(bf16)
        lower = (values - upper.astype(f32)).astype(bf16)
        own = lax.rem(lax.broadcasted_iota(jnp.int32, shape, 0), modes)
        other = lax.rem(lax.broadcasted_iota(jnp.int32, shape, 1), modes)
        same = own == other
        for n, part in enumerate((upper, lower)):
            wide = jnp.dot(part, pick, preferred_element_type=f32)
            target[n] = jnp.where(same, wide, 0.0).astype(bf16)

    def place(k, line, wide, before, after):
        at = pl.ds(line * pad, pad)
        left = jnp.where(spot == 0, before, pltpu.roll(wide, 1, 0))
        right = jnp.where(spot == cols - 1, after, pltpu.roll(wide, pad - 1, 0))
        taps[k, 0, at, :] = left.astype(bf16)
        taps[k, 2, at, :] = right.astype(bf16)

    for k in range(2):
        gain = gain_ref[k : k + 1, :]
        for r in range(rows):
            value = state[r]
            scale = lax.rsqrt(jnp.mean(value * value, axis=-1, keepdims=True) + epsilon)
            normed = (value * scale * gain).astype(bf16)
            taps[k, 1, pl.ds((r + 1) * pad, pad), :] = normed
            wide = normed.astype(f32)
            col_send[k, 0, pl.ds(r, 1), :] = wide[0:1]
            col_send[k, 1, pl.ds(r, 1), :] = wide[cols - 1 : cols]
        if k == 0:
            pl.semaphore_wait(barrier, len(greeted))
        routes = [
            (taps.at[k, 1, pl.ds(pad, pad)], row_recv.at[k, 1]),
            (taps.at[k, 1, pl.ds(rows * pad, pad)], row_recv.at[k, 0]),
            (col_send.at[k, 0], col_recv.at[k, 1]),
            (col_send.at[k, 1], col_recv.at[k, 0]),
            (col_send.at[k, 0, pl.ds(0, 8)], corners.at[k, 0]),
            (col_send.at[k, 0, pl.ds(col_rows - 8, 8)], corners.at[k, 1]),
            (col_send.at[k, 1, pl.ds(0, 8)], corners.at[k, 2]),
            (col_send.at[k, 1, pl.ds(col_rows - 8, 8)], corners.at[k, 3]),
        ]
        copies = []
        for n, (source, target) in enumerate(routes):
            copies.append(
                pltpu.make_async_remote_copy(
                    src_ref=source, dst_ref=target,
                    send_sem=send_sem.at[k, n], recv_sem=recv_sem.at[k, n],
                    device_id=around[n], device_id_type=MESH,
                )
            )
        for n in (4, 5, 6, 7, 0, 1, 2, 3):
            copies[n].start()
        if k == 0:
            legendre()
            own_rows = pl.ds(pl.multiple_of(lat * degrees * modes, 8), degrees * modes)
            expand(basis[own_rows, :] * line_ref[1:2, :], 0, analysis)
        else:
            expand(basis[...], lat * rows, rebuild)
        loads[k].wait()
        for copy in copies:
            copy.wait()
        for r in range(rows):
            place(
                k, r + 1, taps[k, 1, pl.ds((r + 1) * pad, pad), :].astype(f32),
                col_recv[k, 0, pl.ds(r, 1), :], col_recv[k, 1, pl.ds(r, 1), :],
            )
        low = rows - 1 - (col_rows - 8)
        for side, line, inside, west_at, east_at, row in (
            (0, 0, lat > 0, 3, 1, low),
            (1, rows + 1, lat < lat_parts - 1, 2, 0, 0),
        ):
            wide = jnp.where(inside, row_recv[k, side].astype(f32), 0.0)
            taps[k, 1, pl.ds(line * pad, pad), :] = wide.astype(bf16)
            place(
                k, line, wide,
                jnp.where(inside, corners[k, west_at, pl.ds(row, 1), :], 0.0),
                jnp.where(inside, corners[k, east_at, pl.ds(row, 1), :], 0.0),
            )
        total = jnp.zeros((rows * pad, channels), f32)
        for a in range(3):
            for b in range(3):
                total = total + jnp.dot(
                    taps[k, b, pl.ds(a * pad, rows * pad), :], weights[k, a, b],
                    preferred_element_type=f32,
                )
        fresh = state[...].reshape(rows * pad, channels) + gelu(total)
        state[...] = fresh.reshape(rows, pad, channels)

    def cells(g):
        first, last, per = groups[g]
        for i in range(rows):
            for c in range(first, last):
                part, tile = divmod(i * (last - first) + c - first, per)
                yield i, c, part, pl.ds(tile * LANES, LANES)

    def width(g):
        first, last, per = groups[g]
        return pl.ds(first * LANES, (last - first) * LANES)

    def chunk(g, part):
        size = groups[g][2] * LANES
        return pl.ds(pl.multiple_of(part * size, LANES), size)

    def scatter(phase, g, source_of, target):
        copies = []
        for s, peer in enumerate(lon_peers):
            copies.append(
                pltpu.make_async_remote_copy(
                    src_ref=source_of(peer), dst_ref=target.at[lon],
                    send_sem=lon_send.at[phase, g, s], recv_sem=lon_recv.at[phase, g, s],
                    device_id=(lat, peer), device_id_type=MESH,
                )
            )
            copies[-1].start()
        return copies

    def spread(phase, g, buffer):
        copies = []
        for s, peer in enumerate(lat_peers):
            copies.append(
                pltpu.make_async_remote_copy(
                    src_ref=buffer.at[lat], dst_ref=buffer.at[lat],
                    send_sem=lat_send.at[phase, g, s], recv_sem=lat_recv.at[phase, g, s],
                    device_id=(peer, lon), device_id_type=MESH,
                )
            )
            copies[-1].start()
        return copies

    def finish(copies):
        for copy in copies:
            copy.wait_recv()
        started.extend(copies)

    def both(table, data):
        first = jnp.dot(table[0], data, preferred_element_type=f32)
        return first + jnp.dot(table[1], data, preferred_element_type=f32)

    started = []
    every = range(len(groups))
    moving = []
    for g in every:
        first, last, per = groups[g]
        used = rows * (last - first) * LANES
        for i in range(rows):
            for c in range(first, last):
                spot_at = (i * (last - first) + c - first) * LANES
                flat[g][:, pl.ds(spot_at, LANES)] = jnp.where(
                    spot[:, :LANES] < cols, state[i, :, pl.ds(c * LANES, LANES)], 0.0
                ).astype(bf16)
        tail = flat[g].shape[1] - used
        if tail:
            flat[g][:, pl.ds(used, tail)] = jnp.zeros((pad, tail), bf16)
        moving.append(scatter(0, g, lambda peer: flat[g].at[:, chunk(g, peer)], columns[g]))
        columns[g][lon] = flat[g][:, chunk(g, lon)]
    for g in every:
        finish(moving[g])
        spectrum = both(fwd_ref, columns[g][...].reshape(lon_parts * pad, -1))
        spec_out[g][...] = spectrum.astype(bf16).reshape(spec_out[g].shape)
        moving[g] = scatter(1, g, lambda peer: spec_out[g].at[peer], spec_in[g])
        spec_in[g][lon] = spec_out[g][lon]
    for g in every:
        finish(moving[g])
        for i, c, part, at in cells(g):
            piece = spec_in[g][part, :, at].astype(f32)
            packed[pl.ds(i * modes, modes), pl.ds(c * LANES, LANES)] = piece[:modes]
        lat_spec[g][lat] = packed[pl.ds(0, rows * modes), width(g)].astype(bf16)
        moving[g] = spread(0, g, lat_spec[g])
    shape = (modes, keep_ref.shape[1])
    order = 2 * lax.broadcasted_iota(jnp.int32, shape, 1)
    mode = lax.broadcasted_iota(jnp.int32, shape, 0)
    mine = (mode >= order) & (mode < order + 2)
    for g in every:
        finish(moving[g])
        gathered = lat_spec[g][...].reshape(total_rows * modes, -1)
        packed[pl.ds(0, degrees * modes), width(g)] = both(analysis, gathered)
    loads[2].wait()
    for l in range(degrees):
        at = pl.ds(l * modes, modes)
        kept = jnp.where(mine, keep_ref[l : l + 1, :].astype(f32), 0.0)
        kept = jnp.sum(kept, axis=1, keepdims=True)
        mixed[at, :] = jnp.broadcast_to(kept, (modes, channels))
    for g in every:
        for l in range(degrees):
            at = pl.ds(l * modes, modes)
            product = jnp.dot(
                packed[at, :].astype(bf16), fw[l, :, width(g)], preferred_element_type=f32
            )
            mixed[at, width(g)] = product * mixed[at, width(g)]
        lat_filt[g][lat] = mixed[pl.ds(0, degrees * modes), width(g)].astype(bf16)
        moving[g] = spread(1, g, lat_filt[g])
    over = (((0,), (0,)), ((), ()))
    packed[pl.ds(rows * modes, mode_pad), :] = jnp.zeros((mode_pad, channels), f32)
    for g in every:
        finish(moving[g])
        filtered = lat_filt[g][...].reshape(total_degrees * modes, -1)
        packed[pl.ds(0, rows * modes), width(g)] = sum(
            lax.dot_general(rebuild[n], filtered, over, preferred_element_type=f32)
            for n in range(2)
        )
        syn_out[g][...] = jnp.zeros(syn_out[g].shape, bf16)
        for i, c, part, at in cells(g):
            syn_out[g][part, :, at] = packed[
                pl.ds(i * modes, mode_pad), pl.ds(c * LANES, LANES)
            ].astype(bf16)
        moving[g] = scatter(2, g, lambda peer: syn_out[g].at[peer], syn_in[g])
        syn_in[g][lon] = syn_out[g][lon]
    for g in every:
        finish(moving[g])
        physical = both(inv_ref, syn_in[g][...].reshape(lon_parts * mode_pad, -1))
        phys_out[g][...] = physical.astype(bf16).reshape(phys_out[g].shape)
        moving[g] = scatter(3, g, lambda peer: phys_out[g].at[peer], phys_in[g])
        phys_in[g][lon] = phys_out[g][lon]
    for g in every:
        finish(moving[g])
        for i, c, part, at in cells(g):
            here = pl.ds(c * LANES, LANES)
            value = phys_in[g][part, :, at].astype(f32)
            out_ref[i, :, here] = (state[i, :, here] + gelu(value))[:cols]
    for copy in started:
        copy.wait_send()


def per_device(grid_state, norm_gain, conv_weight, filter_weight, degree_keep):
    rows, cols, channels = grid_state.shape
    lat_parts, lon_parts = lax.axis_size("lat"), lax.axis_size("lon")
    degrees, orders = degree_keep.shape
    modes = 2 * orders
    col_pad, mode_pad = up(cols, 16), up(modes, 16)
    col_rows = up(rows, 8)
    tiles = channels // LANES
    middle = (2 * tiles + 2) // 3
    groups = tuple(
        (first, last, -(-rows * (last - first) // lon_parts))
        for first, last in ((0, middle), (middle, tiles))
        if last > first
    )
    total_rows, total_degrees = rows * lat_parts, degrees * lat_parts
    vmem = pl.BlockSpec(memory_space=pltpu.VMEM)
    hbm = pl.BlockSpec(memory_space=pl.ANY)
    dma = pltpu.SemaphoreType.DMA
    forward, inverse = fourier_tables(lon_parts, cols, col_pad, orders, mode_pad)
    seeds, lines = legendre_seeds(lon_parts, orders, modes, total_degrees, total_rows)

    def each(shape_of):
        return tuple(
            pltpu.VMEM(shape_of(per * LANES, (last - first) * LANES), bf16)
            for first, last, per in groups
        )

    block = each(lambda chunk, width: (lon_parts, mode_pad, chunk))
    column_block = each(lambda chunk, width: (lon_parts, col_pad, chunk))
    return pl.pallas_call(
        functools.partial(block_kernel, lat_parts, lon_parts, groups, modes),
        out_shape=jax.ShapeDtypeStruct((rows, cols, channels), f32),
        in_specs=[vmem] * 7 + [hbm, hbm],
        out_specs=vmem,
        scratch_shapes=[
            pltpu.VMEM((rows, col_pad, channels), f32),
            pltpu.VMEM((2, 3, (rows + 2) * col_pad, channels), bf16),
            pltpu.VMEM((2, 3, 3, channels, channels), bf16),
            pltpu.VMEM((2, 2, col_rows, channels), f32),
            pltpu.VMEM((2, 2, col_rows, channels), f32),
            pltpu.VMEM((2, 2, col_pad, channels), bf16),
            pltpu.VMEM((2, 4, 8, channels), f32),
            each(lambda chunk, width: (col_pad, lon_parts * chunk)),
            column_block,
            block,
            block,
            each(lambda chunk, width: (lat_parts, rows * modes, width)),
            each(lambda chunk, width: (lat_parts, degrees * modes, width)),
            block,
            block,
            column_block,
            column_block,
            pltpu.VMEM((total_degrees * modes, total_rows), f32),
            pltpu.VMEM((2, degrees * modes, total_rows * modes), bf16),
            pltpu.VMEM((2, total_degrees * modes, rows * modes), bf16),
            pltpu.VMEM((max(rows, degrees) * modes + mode_pad, channels), f32),
            pltpu.VMEM((degrees * modes, channels), f32),
            pltpu.VMEM((degrees, channels, channels), bf16),
            dma((2,)),
            dma(()),
            dma((2, 8)),
            dma((2, 8)),
            dma((4, len(groups), lon_parts - 1)),
            dma((4, len(groups), lon_parts - 1)),
            dma((2, len(groups), lat_parts - 1)),
            dma((2, len(groups), lat_parts - 1)),
        ],
        compiler_params=pltpu.CompilerParams(collective_id=0, has_side_effects=True),
        name="block",
    )(
        grid_state, norm_gain, degree_keep, jnp.asarray(forward), jnp.asarray(inverse),
        jnp.asarray(seeds), jnp.asarray(lines), conv_weight, filter_weight,
    )


def solution(mesh):
    in_specs = (P("lat", "lon", None), P(), P(), P("lat", None, None), P("lat", "lon"))
    out_specs = P("lat", "lon", None)
    return jax.shard_map(
        per_device, mesh=mesh, in_specs=in_specs, out_specs=out_specs, check_vma=False
    )
```

```python
import functools
import math

import jax
import jax.numpy as jnp
import ml_dtypes
import numpy as np
from jax import lax
from jax.experimental import pallas as pl
from jax.experimental.pallas import tpu as pltpu
from jax.sharding import PartitionSpec as P

epsilon = 1e-06
LANES = 128
MESH = pl.DeviceIdType.MESH
f32 = jnp.float32
bf16 = jnp.bfloat16


def up(value, step):
    return -(-value // step) * step


def gelu(value):
    return 0.5 * value * (1.0 + lax.erf(value * math.sqrt(0.5)))


def split(table):
    upper = table.astype(ml_dtypes.bfloat16)
    lower = (table - upper.astype(np.float64)).astype(ml_dtypes.bfloat16)
    return np.stack([upper, lower])


def fourier_tables(lon_parts, cols, col_pad, orders, mode_pad):
    total = lon_parts * cols
    forward = np.zeros((lon_parts, mode_pad, lon_parts, col_pad))
    inverse = np.zeros((lon_parts, col_pad, lon_parts, mode_pad))
    m = np.arange(lon_parts * orders)[:, None]
    j = np.arange(total)[None, :]
    phase = (m * j % total) * (2.0 * math.pi / total)
    pair = np.stack([np.cos(phase), -np.sin(phase)], axis=1)
    pair = pair.reshape(lon_parts, 2 * orders, lon_parts, cols)
    weight = np.where(m == 0, 1.0, 2.0)[:, :, None]
    back = (np.stack([np.cos(phase), -np.sin(phase)], axis=1) * weight).reshape(pair.shape)
    forward[:, : 2 * orders, :, :cols] = pair * (2.0 * math.pi / total)
    inverse[:, :cols, :, : 2 * orders] = back.transpose(2, 3, 0, 1)
    side_m, side_c = lon_parts * mode_pad, lon_parts * col_pad
    return split(forward.reshape(side_m, side_c)), split(inverse.reshape(side_c, side_m))


def legendre_seeds(lon_parts, orders, mode_pad, degrees, rows):
    count = lon_parts * orders
    m = np.arange(count, dtype=np.float64)[:, None]
    l = np.arange(degrees, dtype=np.float64)[None, :]
    theta = (np.arange(rows) + 0.5) * (math.pi / rows)
    gammas = np.array([math.lgamma(v + 0.5) - math.lgamma(v + 1.0) for v in range(count)])
    log_start = 0.5 * (
        np.log((2.0 * m + 1.0) / (4.0 * math.pi)) + gammas[:, None] - 0.5 * math.log(math.pi)
    ) + m * np.log(np.sin(theta))[None, :]
    growth = np.where(
        l > m, np.sqrt(np.maximum(4 * l * l - 1, 1) / np.maximum(l * l - m * m, 1)), 0.0
    )
    prior = l - 1.0
    damping = np.sqrt(
        np.maximum(prior * prior - m * m, 0) / np.maximum(4 * prior * prior - 1, 1)
    )
    table = np.concatenate([growth, damping, (l == m) * 1.0, np.exp(log_start)], axis=1)
    table = np.repeat(table.reshape(lon_parts, orders, -1), 2, axis=1)
    full = np.zeros((lon_parts, up(mode_pad, 8), table.shape[2]), np.float32)
    full[:, : 2 * orders] = table
    lines = np.stack([np.cos(theta), np.sin(theta) * (math.pi / rows)]).astype(np.float32)
    return full, np.concatenate([lines, np.zeros((6, rows), np.float32)])


def block_kernel(
    lat_parts, lon_parts, groups, modes,
    x_hbm, gain_hbm, keep_hbm, fwd_hbm, inv_hbm, seed_hbm, line_hbm, w_hbm, fw_hbm, out_ref,
    x_ref, gain_ref, keep_ref, fwd_ref, inv_ref, seed_ref, line_ref,
    state, taps, weights, col_send, col_recv, row_recv, corners, flat,
    columns, spec_out, spec_in, lat_spec, lat_filt, syn_out, syn_in, phys_out, phys_in,
    basis, analysis, rebuild, packed, mixed, fw,
    in_sem, w_sem, fw_sem, send_sem, recv_sem, lon_send, lon_recv, lat_send, lat_recv,
):
    rows, cols, channels = x_ref.shape
    pad = state.shape[1]
    mode_pad = spec_in[0].shape[1]
    col_rows = col_send.shape[2]
    degrees = fw.shape[0]
    total_rows = rows * lat_parts
    total_degrees = degrees * lat_parts
    lat, lon = lax.axis_index("lat"), lax.axis_index("lon")
    north = lax.rem(lat + lat_parts - 1, lat_parts)
    south = lax.rem(lat + 1, lat_parts)
    west = lax.rem(lon + lon_parts - 1, lon_parts)
    east = lax.rem(lon + 1, lon_parts)
    lon_peers = [lax.rem(lon + s, lon_parts) for s in range(1, lon_parts)]
    lat_peers = [lax.rem(lat + s, lat_parts) for s in range(1, lat_parts)]
    if lat_parts == 4:
        lat_peers = [
            3 - lat, lat + 1 - 2 * lax.rem(lat, 2), lax.rem(lat + 2, 4),
        ]
    far_first = []
    for n in range(lon_parts - 1):
        down, rise = lon_parts - 1 - n, n
        down = jnp.where(down <= lon, down - 1, down)
        rise = jnp.where(rise >= lon, rise + 1, rise)
        far_first.append(jnp.where(2 * lon < lon_parts, down, rise))
    corner_peers = [(north, west), (south, west), (north, east), (south, east)]
    around = [(north, lon), (south, lon), (lat, west), (lat, east)] + corner_peers
    greeted = [(lat, peer) for peer in lon_peers] + [(peer, lon) for peer in lat_peers]
    greeted += corner_peers
    barrier = pltpu.get_barrier_semaphore()
    for device in greeted:
        pl.semaphore_signal(barrier, inc=1, device_id=device, device_id_type=MESH)
    pairs = [
        (x_hbm, x_ref), (gain_hbm, gain_ref), (seed_hbm.at[lon], seed_ref),
        (line_hbm, line_ref), (fwd_hbm, fwd_ref), (keep_hbm, keep_ref), (inv_hbm, inv_ref),
    ]
    inputs = [
        pltpu.make_async_copy(source, target, in_sem.at[n])
        for n, (source, target) in enumerate(pairs)
    ]
    loads = [
        pltpu.make_async_copy(w_hbm.at[k], weights.at[k], w_sem.at[k]) for k in range(2)
    ]
    loads.append(pltpu.make_async_copy(fw_hbm, fw, fw_sem))
    for load in inputs + loads:
        load.start()
    spot = lax.broadcasted_iota(jnp.int32, (pad, channels), 0)
    col_send[...] = jnp.zeros(col_send.shape, f32)
    for load in inputs[:2]:
        load.wait()
    for r in range(rows):
        state[r, pl.ds(cols, pad - cols), :] = jnp.zeros((pad - cols, channels), f32)
        state[r, pl.ds(0, cols), :] = x_ref[r]

    def legendre():
        seeds = seed_ref[...]
        growth = seeds[:, :total_degrees]
        damping = seeds[:, total_degrees : 2 * total_degrees]
        start = seeds[:, 2 * total_degrees : 3 * total_degrees]
        sectoral = seeds[:, 3 * total_degrees :]
        cosine = line_ref[0:1, :]
        before = jnp.zeros(sectoral.shape, f32)
        latest = before
        for l in range(total_degrees):
            grown = growth[:, l : l + 1] * (cosine * latest - damping[:, l : l + 1] * before)
            before, latest = latest, grown + start[:, l : l + 1] * sectoral
            basis[pl.ds(l * modes, modes), :] = latest[:modes]

    def expand(values, first_row, target):
        shape = target.shape[1:]
        row = lax.broadcasted_iota(jnp.int32, (total_rows, shape[1]), 0) * modes
        at = lax.broadcasted_iota(jnp.int32, (total_rows, shape[1]), 1) + first_row * modes
        pick = jnp.where((at >= row) & (at < row + modes), 1.0, 0.0).astype(bf16)
        upper = values.astype(bf16)
        lower = (values - upper.astype(f32)).astype(bf16)
        own = lax.rem(lax.broadcasted_iota(jnp.int32, shape, 0), modes)
        other = lax.rem(lax.broadcasted_iota(jnp.int32, shape, 1), modes)
        same = own == other
        for n, part in enumerate((upper, lower)):
            wide = jnp.dot(part, pick, preferred_element_type=f32)
            target[n] = jnp.where(same, wide, 0.0).astype(bf16)

    def place(k, line, wide, before, after):
        at = pl.ds(line * pad, pad)
        left = jnp.where(spot == 0, before, pltpu.roll(wide, 1, 0))
        right = jnp.where(spot == cols - 1, after, pltpu.roll(wide, pad - 1, 0))
        taps[k, 0, at, :] = left.astype(bf16)
        taps[k, 2, at, :] = right.astype(bf16)

    for k in range(2):
        gain = gain_ref[k : k + 1, :]
        for r in range(rows):
            value = state[r]
            scale = lax.rsqrt(jnp.mean(value * value, axis=-1, keepdims=True) + epsilon)
            normed = (value * scale * gain).astype(bf16)
            taps[k, 1, pl.ds((r + 1) * pad, pad), :] = normed
            wide = normed.astype(f32)
            col_send[k, 0, pl.ds(r, 1), :] = wide[0:1]
            col_send[k, 1, pl.ds(r, 1), :] = wide[cols - 1 : cols]
        if k == 0:
            pl.semaphore_wait(barrier, len(greeted))
        routes = [
            (taps.at[k, 1, pl.ds(pad, pad)], row_recv.at[k, 1]),
            (taps.at[k, 1, pl.ds(rows * pad, pad)], row_recv.at[k, 0]),
            (col_send.at[k, 0], col_recv.at[k, 1]),
            (col_send.at[k, 1], col_recv.at[k, 0]),
            (col_send.at[k, 0, pl.ds(0, 8)], corners.at[k, 0]),
            (col_send.at[k, 0, pl.ds(col_rows - 8, 8)], corners.at[k, 1]),
            (col_send.at[k, 1, pl.ds(0, 8)], corners.at[k, 2]),
            (col_send.at[k, 1, pl.ds(col_rows - 8, 8)], corners.at[k, 3]),
        ]
        copies = []
        for n, (source, target) in enumerate(routes):
            copies.append(
                pltpu.make_async_remote_copy(
                    src_ref=source, dst_ref=target,
                    send_sem=send_sem.at[k, n], recv_sem=recv_sem.at[k, n],
                    device_id=around[n], device_id_type=MESH,
                )
            )
        for n in (4, 5, 6, 7, 0, 1, 2, 3):
            copies[n].start()
        if k == 0:
            for load in inputs[2:]:
                load.wait()
            legendre()
            own_rows = pl.ds(pl.multiple_of(lat * degrees * modes, 8), degrees * modes)
            expand(basis[own_rows, :] * line_ref[1:2, :], 0, analysis)
        else:
            expand(basis[...], lat * rows, rebuild)
        loads[k].wait()
        for copy in copies:
            copy.wait()
        for r in range(rows):
            place(
                k, r + 1, taps[k, 1, pl.ds((r + 1) * pad, pad), :].astype(f32),
                col_recv[k, 0, pl.ds(r, 1), :], col_recv[k, 1, pl.ds(r, 1), :],
            )
        low = rows - 1 - (col_rows - 8)
        for side, line, inside, west_at, east_at, row in (
            (0, 0, lat > 0, 3, 1, low),
            (1, rows + 1, lat < lat_parts - 1, 2, 0, 0),
        ):
            wide = jnp.where(inside, row_recv[k, side].astype(f32), 0.0)
            taps[k, 1, pl.ds(line * pad, pad), :] = wide.astype(bf16)
            place(
                k, line, wide,
                jnp.where(inside, corners[k, west_at, pl.ds(row, 1), :], 0.0),
                jnp.where(inside, corners[k, east_at, pl.ds(row, 1), :], 0.0),
            )
        total = jnp.zeros((rows * pad, channels), f32)
        for a in range(3):
            for b in range(3):
                total = total + jnp.dot(
                    taps[k, b, pl.ds(a * pad, rows * pad), :], weights[k, a, b],
                    preferred_element_type=f32,
                )
        fresh = state[...].reshape(rows * pad, channels) + gelu(total)
        state[...] = fresh.reshape(rows, pad, channels)

    def cells(g):
        first, last, per = groups[g]
        for i in range(rows):
            for c in range(first, last):
                part, tile = divmod(i * (last - first) + c - first, per)
                yield i, c, part, pl.ds(tile * LANES, LANES)

    def width(g):
        first, last, per = groups[g]
        return pl.ds(first * LANES, (last - first) * LANES)

    def chunk(g, part):
        size = groups[g][2] * LANES
        return pl.ds(pl.multiple_of(part * size, LANES), size)

    def scatter(phase, g, source_of, target):
        sends = [
            pltpu.make_async_remote_copy(
                src_ref=source_of(peer), dst_ref=target.at[lon],
                send_sem=lon_send.at[phase, g, s], recv_sem=lon_recv.at[phase, g, lon],
                device_id=(lat, peer), device_id_type=MESH,
            )
            for s, peer in enumerate(far_first)
        ]
        for copy in sends:
            copy.start()
        started.extend(sends)
        return [
            pltpu.make_async_remote_copy(
                src_ref=target.at[peer], dst_ref=target.at[peer],
                send_sem=lon_send.at[phase, g, s], recv_sem=lon_recv.at[phase, g, peer],
                device_id=(lat, peer), device_id_type=MESH,
            )
            for s, peer in enumerate(lon_peers)
        ]

    def spread(phase, g, buffer):
        copies = []
        for s, peer in enumerate(lat_peers):
            copies.append(
                pltpu.make_async_remote_copy(
                    src_ref=buffer.at[lat], dst_ref=buffer.at[lat],
                    send_sem=lat_send.at[phase, g, s], recv_sem=lat_recv.at[phase, g, s],
                    device_id=(peer, lon), device_id_type=MESH,
                )
            )
            copies[-1].start()
        started.extend(copies)
        return copies

    def finish(copies):
        for copy in copies:
            copy.wait_recv()

    def both(table, data):
        first = jnp.dot(table[0], data, preferred_element_type=f32)
        return first + jnp.dot(table[1], data, preferred_element_type=f32)

    started = []
    every = range(len(groups))
    moving = []
    for g in every:
        first, last, per = groups[g]
        used = rows * (last - first) * LANES
        for i in range(rows):
            for c in range(first, last):
                spot_at = (i * (last - first) + c - first) * LANES
                flat[g][:, pl.ds(spot_at, LANES)] = jnp.where(
                    spot[:, :LANES] < cols, state[i, :, pl.ds(c * LANES, LANES)], 0.0
                ).astype(bf16)
        tail = flat[g].shape[1] - used
        if tail:
            flat[g][:, pl.ds(used, tail)] = jnp.zeros((pad, tail), bf16)
        moving.append(scatter(0, g, lambda peer: flat[g].at[:, chunk(g, peer)], columns[g]))
        columns[g][lon] = flat[g][:, chunk(g, lon)]
    for g in every:
        finish(moving[g])
        spectrum = both(fwd_ref, columns[g][...].reshape(lon_parts * pad, -1))
        spec_out[g][...] = spectrum.astype(bf16).reshape(spec_out[g].shape)
        moving[g] = scatter(1, g, lambda peer: spec_out[g].at[peer], spec_in[g])
        spec_in[g][lon] = spec_out[g][lon]
    for g in every:
        finish(moving[g])
        for i, c, part, at in cells(g):
            piece = spec_in[g][part, :, at].astype(f32)
            packed[pl.ds(i * modes, modes), pl.ds(c * LANES, LANES)] = piece[:modes]
        lat_spec[g][lat] = packed[pl.ds(0, rows * modes), width(g)].astype(bf16)
        moving[g] = spread(0, g, lat_spec[g])
    shape = (modes, keep_ref.shape[1])
    order = 2 * lax.broadcasted_iota(jnp.int32, shape, 1)
    mode = lax.broadcasted_iota(jnp.int32, shape, 0)
    mine = (mode >= order) & (mode < order + 2)
    for g in every:
        finish(moving[g])
        gathered = lat_spec[g][...].reshape(total_rows * modes, -1)
        packed[pl.ds(0, degrees * modes), width(g)] = both(analysis, gathered)
    loads[2].wait()
    for l in range(degrees):
        at = pl.ds(l * modes, modes)
        kept = jnp.where(mine, keep_ref[l : l + 1, :].astype(f32), 0.0)
        kept = jnp.sum(kept, axis=1, keepdims=True)
        mixed[at, :] = jnp.broadcast_to(kept, (modes, channels))
    for g in every:
        for l in range(degrees):
            at = pl.ds(l * modes, modes)
            product = jnp.dot(
                packed[at, :].astype(bf16), fw[l, :, width(g)], preferred_element_type=f32
            )
            mixed[at, width(g)] = product * mixed[at, width(g)]
        lat_filt[g][lat] = mixed[pl.ds(0, degrees * modes), width(g)].astype(bf16)
        moving[g] = spread(1, g, lat_filt[g])
    over = (((0,), (0,)), ((), ()))
    packed[pl.ds(rows * modes, mode_pad), :] = jnp.zeros((mode_pad, channels), f32)
    for g in every:
        finish(moving[g])
        filtered = lat_filt[g][...].reshape(total_degrees * modes, -1)
        packed[pl.ds(0, rows * modes), width(g)] = sum(
            lax.dot_general(rebuild[n], filtered, over, preferred_element_type=f32)
            for n in range(2)
        )
        syn_out[g][...] = jnp.zeros(syn_out[g].shape, bf16)
        for i, c, part, at in cells(g):
            syn_out[g][part, :, at] = packed[
                pl.ds(i * modes, mode_pad), pl.ds(c * LANES, LANES)
            ].astype(bf16)
        moving[g] = scatter(2, g, lambda peer: syn_out[g].at[peer], syn_in[g])
        syn_in[g][lon] = syn_out[g][lon]
    for g in every:
        finish(moving[g])
        physical = both(inv_ref, syn_in[g][...].reshape(lon_parts * mode_pad, -1))
        phys_out[g][...] = physical.astype(bf16).reshape(phys_out[g].shape)
        moving[g] = scatter(3, g, lambda peer: phys_out[g].at[peer], phys_in[g])
        phys_in[g][lon] = phys_out[g][lon]
    for g in every:
        finish(moving[g])
        for i, c, part, at in cells(g):
            here = pl.ds(c * LANES, LANES)
            value = phys_in[g][part, :, at].astype(f32)
            out_ref[i, :, here] = (state[i, :, here] + gelu(value))[:cols]
    for copy in started:
        copy.wait_send()


def per_device(grid_state, norm_gain, conv_weight, filter_weight, degree_keep):
    rows, cols, channels = grid_state.shape
    lat_parts, lon_parts = lax.axis_size("lat"), lax.axis_size("lon")
    degrees, orders = degree_keep.shape
    modes = 2 * orders
    col_pad, mode_pad = up(cols, 16), up(modes, 16)
    col_rows = up(rows, 8)
    tiles = channels // LANES
    middle = (2 * tiles + 2) // 3
    groups = tuple(
        (first, last, -(-rows * (last - first) // lon_parts))
        for first, last in ((0, middle), (middle, tiles))
        if last > first
    )
    total_rows, total_degrees = rows * lat_parts, degrees * lat_parts
    vmem = pl.BlockSpec(memory_space=pltpu.VMEM)
    hbm = pl.BlockSpec(memory_space=pl.ANY)
    dma = pltpu.SemaphoreType.DMA
    forward, inverse = fourier_tables(lon_parts, cols, col_pad, orders, mode_pad)
    seeds, lines = legendre_seeds(lon_parts, orders, modes, total_degrees, total_rows)

    def each(shape_of):
        return tuple(
            pltpu.VMEM(shape_of(per * LANES, (last - first) * LANES), bf16)
            for first, last, per in groups
        )

    block = each(lambda chunk, width: (lon_parts, mode_pad, chunk))
    column_block = each(lambda chunk, width: (lon_parts, col_pad, chunk))
    return pl.pallas_call(
        functools.partial(block_kernel, lat_parts, lon_parts, groups, modes),
        out_shape=jax.ShapeDtypeStruct((rows, cols, channels), f32),
        in_specs=[hbm] * 9,
        out_specs=vmem,
        scratch_shapes=[
            pltpu.VMEM((rows, cols, channels), f32),
            pltpu.VMEM(norm_gain.shape, f32),
            pltpu.VMEM(degree_keep.shape, degree_keep.dtype),
            pltpu.VMEM(forward.shape, bf16),
            pltpu.VMEM(inverse.shape, bf16),
            pltpu.VMEM(seeds.shape[1:], f32),
            pltpu.VMEM(lines.shape, f32),
            pltpu.VMEM((rows, col_pad, channels), f32),
            pltpu.VMEM((2, 3, (rows + 2) * col_pad, channels), bf16),
            pltpu.VMEM((2, 3, 3, channels, channels), bf16),
            pltpu.VMEM((2, 2, col_rows, channels), f32),
            pltpu.VMEM((2, 2, col_rows, channels), f32),
            pltpu.VMEM((2, 2, col_pad, channels), bf16),
            pltpu.VMEM((2, 4, 8, channels), f32),
            each(lambda chunk, width: (col_pad, lon_parts * chunk)),
            column_block,
            block,
            block,
            each(lambda chunk, width: (lat_parts, rows * modes, width)),
            each(lambda chunk, width: (lat_parts, degrees * modes, width)),
            block,
            block,
            column_block,
            column_block,
            pltpu.VMEM((total_degrees * modes, total_rows), f32),
            pltpu.VMEM((2, degrees * modes, total_rows * modes), bf16),
            pltpu.VMEM((2, total_degrees * modes, rows * modes), bf16),
            pltpu.VMEM((max(rows, degrees) * modes + mode_pad, channels), f32),
            pltpu.VMEM((degrees * modes, channels), f32),
            pltpu.VMEM((degrees, channels, channels), bf16),
            dma((7,)),
            dma((2,)),
            dma(()),
            dma((2, 8)),
            dma((2, 8)),
            dma((4, len(groups), lon_parts - 1)),
            dma((4, len(groups), lon_parts)),
            dma((2, len(groups), lat_parts - 1)),
            dma((2, len(groups), lat_parts - 1)),
        ],
        compiler_params=pltpu.CompilerParams(collective_id=0, has_side_effects=True),
        name="block",
    )(
        grid_state, norm_gain, degree_keep, jnp.asarray(forward), jnp.asarray(inverse),
        jnp.asarray(seeds), jnp.asarray(lines), conv_weight, filter_weight,
    )


def solution(mesh):
    in_specs = (P("lat", "lon", None), P(), P(), P("lat", None, None), P("lat", "lon"))
    out_specs = P("lat", "lon", None)
    return jax.shard_map(
        per_device, mesh=mesh, in_specs=in_specs, out_specs=out_specs, check_vma=False
    )
```

```python
import functools
import math

import jax
import jax.numpy as jnp
import ml_dtypes
import numpy as np
from jax import lax
from jax.experimental import pallas as pl
from jax.experimental.pallas import tpu as pltpu
from jax.sharding import PartitionSpec as P

epsilon = 1e-06
LANES = 128
MESH = pl.DeviceIdType.MESH
f32 = jnp.float32
bf16 = jnp.bfloat16


def up(value, step):
    return -(-value // step) * step


def gelu(value):
    return 0.5 * value * (1.0 + lax.erf(value * math.sqrt(0.5)))


def split(table):
    upper = table.astype(ml_dtypes.bfloat16)
    lower = (table - upper.astype(np.float64)).astype(ml_dtypes.bfloat16)
    return np.stack([upper, lower])


def fourier_tables(lon_parts, cols, col_pad, orders, mode_pad):
    total = lon_parts * cols
    forward = np.zeros((lon_parts, mode_pad, lon_parts, col_pad))
    inverse = np.zeros((lon_parts, col_pad, lon_parts, mode_pad))
    m = np.arange(lon_parts * orders)[:, None]
    j = np.arange(total)[None, :]
    phase = (m * j % total) * (2.0 * math.pi / total)
    pair = np.stack([np.cos(phase), -np.sin(phase)], axis=1)
    pair = pair.reshape(lon_parts, 2 * orders, lon_parts, cols)
    weight = np.where(m == 0, 1.0, 2.0)[:, :, None]
    back = (np.stack([np.cos(phase), -np.sin(phase)], axis=1) * weight).reshape(pair.shape)
    forward[:, : 2 * orders, :, :cols] = pair * (2.0 * math.pi / total)
    inverse[:, :cols, :, : 2 * orders] = back.transpose(2, 3, 0, 1)
    side_m, side_c = lon_parts * mode_pad, lon_parts * col_pad
    return split(forward.reshape(side_m, side_c)), split(inverse.reshape(side_c, side_m))


def legendre_seeds(lon_parts, orders, mode_pad, degrees, rows):
    count = lon_parts * orders
    m = np.arange(count, dtype=np.float64)[:, None]
    l = np.arange(degrees, dtype=np.float64)[None, :]
    theta = (np.arange(rows) + 0.5) * (math.pi / rows)
    gammas = np.array([math.lgamma(v + 0.5) - math.lgamma(v + 1.0) for v in range(count)])
    log_start = 0.5 * (
        np.log((2.0 * m + 1.0) / (4.0 * math.pi)) + gammas[:, None] - 0.5 * math.log(math.pi)
    ) + m * np.log(np.sin(theta))[None, :]
    growth = np.where(
        l > m, np.sqrt(np.maximum(4 * l * l - 1, 1) / np.maximum(l * l - m * m, 1)), 0.0
    )
    prior = l - 1.0
    damping = np.sqrt(
        np.maximum(prior * prior - m * m, 0) / np.maximum(4 * prior * prior - 1, 1)
    )
    table = np.concatenate([growth, damping, (l == m) * 1.0, np.exp(log_start)], axis=1)
    table = np.repeat(table.reshape(lon_parts, orders, -1), 2, axis=1)
    full = np.zeros((lon_parts, up(mode_pad, 8), table.shape[2]), np.float32)
    full[:, : 2 * orders] = table
    lines = np.stack([np.cos(theta), np.sin(theta) * (math.pi / rows)]).astype(np.float32)
    return full, np.concatenate([lines, np.zeros((6, rows), np.float32)])


def block_kernel(
    lat_parts, lon_parts, groups, modes,
    x_hbm, gain_hbm, keep_hbm, fwd_hbm, inv_hbm, seed_hbm, line_hbm, w_hbm, fw_hbm, out_ref,
    x_ref, gain_ref, keep_ref, fwd_ref, inv_ref, seed_ref, line_ref,
    state, taps, weights, col_send, col_recv, row_recv, corners, flat,
    columns, spec_out, spec_in, lat_spec, lat_filt, syn_out, syn_in, phys_out, phys_in,
    basis, analysis, rebuild, packed, mixed, fw,
    in_sem, w_sem, fw_sem, send_sem, recv_sem, lon_send, lon_recv, lat_send, lat_recv,
):
    rows, cols, channels = x_ref.shape
    pad = state.shape[1]
    mode_pad = spec_in[0].shape[1]
    col_rows = col_send.shape[2]
    degrees = fw.shape[0]
    total_rows = rows * lat_parts
    total_degrees = degrees * lat_parts
    lat, lon = lax.axis_index("lat"), lax.axis_index("lon")
    north = lax.rem(lat + lat_parts - 1, lat_parts)
    south = lax.rem(lat + 1, lat_parts)
    west = lax.rem(lon + lon_parts - 1, lon_parts)
    east = lax.rem(lon + 1, lon_parts)
    lon_peers = [lax.rem(lon + s, lon_parts) for s in range(1, lon_parts)]
    lat_peers = [lax.rem(lat + s, lat_parts) for s in range(1, lat_parts)]
    if lat_parts == 4:
        lat_peers = [
            3 - lat, lat + 1 - 2 * lax.rem(lat, 2), lax.rem(lat + 2, 4),
        ]
    far_first = []
    for n in range(lon_parts - 1):
        down, rise = lon_parts - 1 - n, n
        down = jnp.where(down <= lon, down - 1, down)
        rise = jnp.where(rise >= lon, rise + 1, rise)
        far_first.append(jnp.where(2 * lon < lon_parts, down, rise))
    corner_peers = [(north, west), (south, west), (north, east), (south, east)]
    around = [(north, lon), (south, lon), (lat, west), (lat, east)] + corner_peers
    greeted = [(lat, peer) for peer in lon_peers] + [(peer, lon) for peer in lat_peers]
    greeted += corner_peers
    barrier = pltpu.get_barrier_semaphore()
    for device in greeted:
        pl.semaphore_signal(barrier, inc=1, device_id=device, device_id_type=MESH)
    pairs = [
        (x_hbm, x_ref), (gain_hbm, gain_ref), (seed_hbm.at[lon], seed_ref),
        (line_hbm, line_ref), (fwd_hbm, fwd_ref), (keep_hbm, keep_ref), (inv_hbm, inv_ref),
    ]
    inputs = [
        pltpu.make_async_copy(source, target, in_sem.at[n])
        for n, (source, target) in enumerate(pairs)
    ]
    loads = [
        pltpu.make_async_copy(w_hbm.at[k], weights.at[k], w_sem.at[k]) for k in range(2)
    ]
    loads.append(pltpu.make_async_copy(fw_hbm, fw, fw_sem))
    for load in inputs + loads:
        load.start()
    spot = lax.broadcasted_iota(jnp.int32, (pad, channels), 0)
    col_send[...] = jnp.zeros(col_send.shape, f32)
    for load in inputs[:2]:
        load.wait()
    for r in range(rows):
        state[r, pl.ds(cols, pad - cols), :] = jnp.zeros((pad - cols, channels), f32)
        state[r, pl.ds(0, cols), :] = x_ref[r]

    def legendre():
        seeds = seed_ref[...]
        growth = seeds[:, :total_degrees]
        damping = seeds[:, total_degrees : 2 * total_degrees]
        start = seeds[:, 2 * total_degrees : 3 * total_degrees]
        sectoral = seeds[:, 3 * total_degrees :]
        cosine = line_ref[0:1, :]
        before = jnp.zeros(sectoral.shape, f32)
        latest = before
        for l in range(total_degrees):
            grown = growth[:, l : l + 1] * (cosine * latest - damping[:, l : l + 1] * before)
            before, latest = latest, grown + start[:, l : l + 1] * sectoral
            basis[pl.ds(l * modes, modes), :] = latest[:modes]

    def expand(values, first_row, target):
        shape = target.shape[1:]
        row = lax.broadcasted_iota(jnp.int32, (total_rows, shape[1]), 0) * modes
        at = lax.broadcasted_iota(jnp.int32, (total_rows, shape[1]), 1) + first_row * modes
        pick = jnp.where((at >= row) & (at < row + modes), 1.0, 0.0).astype(bf16)
        upper = values.astype(bf16)
        lower = (values - upper.astype(f32)).astype(bf16)
        own = lax.rem(lax.broadcasted_iota(jnp.int32, shape, 0), modes)
        other = lax.rem(lax.broadcasted_iota(jnp.int32, shape, 1), modes)
        same = own == other
        for n, part in enumerate((upper, lower)):
            wide = jnp.dot(part, pick, preferred_element_type=f32)
            target[n] = jnp.where(same, wide, 0.0).astype(bf16)

    def place(k, line, wide, before, after):
        at = pl.ds(line * pad, pad)
        left = jnp.where(spot == 0, before, pltpu.roll(wide, 1, 0))
        right = jnp.where(spot == cols - 1, after, pltpu.roll(wide, pad - 1, 0))
        taps[k, 0, at, :] = left.astype(bf16)
        taps[k, 2, at, :] = right.astype(bf16)

    for k in range(2):
        gain = gain_ref[k : k + 1, :]
        for r in range(rows):
            value = state[r]
            scale = lax.rsqrt(jnp.mean(value * value, axis=-1, keepdims=True) + epsilon)
            normed = (value * scale * gain).astype(bf16)
            taps[k, 1, pl.ds((r + 1) * pad, pad), :] = normed
            wide = normed.astype(f32)
            col_send[k, 0, pl.ds(r, 1), :] = wide[0:1]
            col_send[k, 1, pl.ds(r, 1), :] = wide[cols - 1 : cols]
        if k == 0:
            pl.semaphore_wait(barrier, len(greeted))
        routes = [
            (taps.at[k, 1, pl.ds(pad, pad)], row_recv.at[k, 1]),
            (taps.at[k, 1, pl.ds(rows * pad, pad)], row_recv.at[k, 0]),
            (col_send.at[k, 0], col_recv.at[k, 1]),
            (col_send.at[k, 1], col_recv.at[k, 0]),
            (col_send.at[k, 0, pl.ds(0, 8)], corners.at[k, 0]),
            (col_send.at[k, 0, pl.ds(col_rows - 8, 8)], corners.at[k, 1]),
            (col_send.at[k, 1, pl.ds(0, 8)], corners.at[k, 2]),
            (col_send.at[k, 1, pl.ds(col_rows - 8, 8)], corners.at[k, 3]),
        ]
        copies = []
        for n, (source, target) in enumerate(routes):
            copies.append(
                pltpu.make_async_remote_copy(
                    src_ref=source, dst_ref=target,
                    send_sem=send_sem.at[k, n], recv_sem=recv_sem.at[k, n],
                    device_id=around[n], device_id_type=MESH,
                )
            )
        for n in (4, 5, 6, 7, 0, 1, 2, 3):
            copies[n].start()
        if k == 0:
            for load in inputs[2:]:
                load.wait()
            legendre()
            own_rows = pl.ds(pl.multiple_of(lat * degrees * modes, 8), degrees * modes)
            expand(basis[own_rows, :] * line_ref[1:2, :], 0, analysis)
        else:
            expand(basis[...], lat * rows, rebuild)
        for r in range(rows):
            at = pl.ds((r + 1) * pad, pad)
            wide = taps[k, 1, at, :].astype(f32)
            taps[k, 0, at, :] = pltpu.roll(wide, 1, 0).astype(bf16)
            taps[k, 2, at, :] = pltpu.roll(wide, pad - 1, 0).astype(bf16)
        loads[k].wait()
        for copy in copies:
            copy.wait()
        for r in range(rows):
            base = (r + 1) * pad
            taps[k, 0, pl.ds(base, 1), :] = col_recv[k, 0, pl.ds(r, 1), :].astype(bf16)
            taps[k, 2, pl.ds(base + cols - 1, 1), :] = col_recv[k, 1, pl.ds(r, 1), :].astype(bf16)
        low = rows - 1 - (col_rows - 8)
        for side, line, inside, west_at, east_at, row in (
            (0, 0, lat > 0, 3, 1, low),
            (1, rows + 1, lat < lat_parts - 1, 2, 0, 0),
        ):
            wide = jnp.where(inside, row_recv[k, side].astype(f32), 0.0)
            taps[k, 1, pl.ds(line * pad, pad), :] = wide.astype(bf16)
            place(
                k, line, wide,
                jnp.where(inside, corners[k, west_at, pl.ds(row, 1), :], 0.0),
                jnp.where(inside, corners[k, east_at, pl.ds(row, 1), :], 0.0),
            )
        total = jnp.zeros((rows * pad, channels), f32)
        for a in range(3):
            for b in range(3):
                total = total + jnp.dot(
                    taps[k, b, pl.ds(a * pad, rows * pad), :], weights[k, a, b],
                    preferred_element_type=f32,
                )
        fresh = state[...].reshape(rows * pad, channels) + gelu(total)
        state[...] = fresh.reshape(rows, pad, channels)

    def cells(g):
        first, last, per = groups[g]
        for i in range(rows):
            for c in range(first, last):
                part, tile = divmod(i * (last - first) + c - first, per)
                yield i, c, part, pl.ds(tile * LANES, LANES)

    def width(g):
        first, last, per = groups[g]
        return pl.ds(first * LANES, (last - first) * LANES)

    def chunk(g, part):
        size = groups[g][2] * LANES
        return pl.ds(pl.multiple_of(part * size, LANES), size)

    def scatter(phase, g, source_of, target):
        sends = [
            pltpu.make_async_remote_copy(
                src_ref=source_of(peer), dst_ref=target.at[lon],
                send_sem=lon_send.at[phase, g, s], recv_sem=lon_recv.at[phase, g, lon],
                device_id=(lat, peer), device_id_type=MESH,
            )
            for s, peer in enumerate(far_first)
        ]
        for copy in sends:
            copy.start()
        started.extend(sends)
        return [
            pltpu.make_async_remote_copy(
                src_ref=target.at[peer], dst_ref=target.at[peer],
                send_sem=lon_send.at[phase, g, s], recv_sem=lon_recv.at[phase, g, peer],
                device_id=(lat, peer), device_id_type=MESH,
            )
            for s, peer in enumerate(lon_peers)
        ]

    def spread(phase, g, buffer):
        copies = []
        for s, peer in enumerate(lat_peers):
            copies.append(
                pltpu.make_async_remote_copy(
                    src_ref=buffer.at[lat], dst_ref=buffer.at[lat],
                    send_sem=lat_send.at[phase, g, s], recv_sem=lat_recv.at[phase, g, s],
                    device_id=(peer, lon), device_id_type=MESH,
                )
            )
            copies[-1].start()
        started.extend(copies)
        return copies

    def finish(copies):
        for copy in copies:
            copy.wait_recv()

    def both(table, data):
        first = jnp.dot(table[0], data, preferred_element_type=f32)
        return first + jnp.dot(table[1], data, preferred_element_type=f32)

    started = []
    every = range(len(groups))
    moving = []
    for g in every:
        first, last, per = groups[g]
        used = rows * (last - first) * LANES
        for i in range(rows):
            for c in range(first, last):
                spot_at = (i * (last - first) + c - first) * LANES
                flat[g][:, pl.ds(spot_at, LANES)] = jnp.where(
                    spot[:, :LANES] < cols, state[i, :, pl.ds(c * LANES, LANES)], 0.0
                ).astype(bf16)
        tail = flat[g].shape[1] - used
        if tail:
            flat[g][:, pl.ds(used, tail)] = jnp.zeros((pad, tail), bf16)
        moving.append(scatter(0, g, lambda peer: flat[g].at[:, chunk(g, peer)], columns[g]))
        columns[g][lon] = flat[g][:, chunk(g, lon)]
    for g in every:
        finish(moving[g])
        spectrum = both(fwd_ref, columns[g][...].reshape(lon_parts * pad, -1))
        spec_out[g][...] = spectrum.astype(bf16).reshape(spec_out[g].shape)
        moving[g] = scatter(1, g, lambda peer: spec_out[g].at[peer], spec_in[g])
        spec_in[g][lon] = spec_out[g][lon]
    for g in every:
        finish(moving[g])
        for i, c, part, at in cells(g):
            piece = spec_in[g][part, :, at].astype(f32)
            packed[pl.ds(i * modes, modes), pl.ds(c * LANES, LANES)] = piece[:modes]
        lat_spec[g][lat] = packed[pl.ds(0, rows * modes), width(g)].astype(bf16)
        moving[g] = spread(0, g, lat_spec[g])
    shape = (modes, keep_ref.shape[1])
    order = 2 * lax.broadcasted_iota(jnp.int32, shape, 1)
    mode = lax.broadcasted_iota(jnp.int32, shape, 0)
    mine = (mode >= order) & (mode < order + 2)
    for g in every:
        finish(moving[g])
        gathered = lat_spec[g][...].reshape(total_rows * modes, -1)
        packed[pl.ds(0, degrees * modes), width(g)] = both(analysis, gathered)
    loads[2].wait()
    for l in range(degrees):
        at = pl.ds(l * modes, modes)
        kept = jnp.where(mine, keep_ref[l : l + 1, :].astype(f32), 0.0)
        kept = jnp.sum(kept, axis=1, keepdims=True)
        mixed[at, :] = jnp.broadcast_to(kept, (modes, channels))
    for g in every:
        for l in range(degrees):
            at = pl.ds(l * modes, modes)
            product = jnp.dot(
                packed[at, :].astype(bf16), fw[l, :, width(g)], preferred_element_type=f32
            )
            mixed[at, width(g)] = product * mixed[at, width(g)]
        lat_filt[g][lat] = mixed[pl.ds(0, degrees * modes), width(g)].astype(bf16)
        moving[g] = spread(1, g, lat_filt[g])
    over = (((0,), (0,)), ((), ()))
    packed[pl.ds(rows * modes, mode_pad), :] = jnp.zeros((mode_pad, channels), f32)
    for g in every:
        finish(moving[g])
        filtered = lat_filt[g][...].reshape(total_degrees * modes, -1)
        packed[pl.ds(0, rows * modes), width(g)] = sum(
            lax.dot_general(rebuild[n], filtered, over, preferred_element_type=f32)
            for n in range(2)
        )
        syn_out[g][...] = jnp.zeros(syn_out[g].shape, bf16)
        for i, c, part, at in cells(g):
            syn_out[g][part, :, at] = packed[
                pl.ds(i * modes, mode_pad), pl.ds(c * LANES, LANES)
            ].astype(bf16)
        moving[g] = scatter(2, g, lambda peer: syn_out[g].at[peer], syn_in[g])
        syn_in[g][lon] = syn_out[g][lon]
    for g in every:
        finish(moving[g])
        physical = both(inv_ref, syn_in[g][...].reshape(lon_parts * mode_pad, -1))
        phys_out[g][...] = physical.astype(bf16).reshape(phys_out[g].shape)
        moving[g] = scatter(3, g, lambda peer: phys_out[g].at[peer], phys_in[g])
        phys_in[g][lon] = phys_out[g][lon]
    for g in every:
        finish(moving[g])
        for i, c, part, at in cells(g):
            here = pl.ds(c * LANES, LANES)
            value = phys_in[g][part, :, at].astype(f32)
            out_ref[i, :, here] = (state[i, :, here] + gelu(value))[:cols]
    for copy in started:
        copy.wait_send()


def per_device(grid_state, norm_gain, conv_weight, filter_weight, degree_keep):
    rows, cols, channels = grid_state.shape
    lat_parts, lon_parts = lax.axis_size("lat"), lax.axis_size("lon")
    degrees, orders = degree_keep.shape
    modes = 2 * orders
    col_pad, mode_pad = up(cols, 16), up(modes, 16)
    col_rows = up(rows, 8)
    tiles = channels // LANES
    middle = tiles // 3
    groups = tuple(
        (first, last, -(-rows * (last - first) // lon_parts))
        for first, last in ((0, middle), (middle, tiles))
        if last > first
    )
    total_rows, total_degrees = rows * lat_parts, degrees * lat_parts
    vmem = pl.BlockSpec(memory_space=pltpu.VMEM)
    hbm = pl.BlockSpec(memory_space=pl.ANY)
    dma = pltpu.SemaphoreType.DMA
    forward, inverse = fourier_tables(lon_parts, cols, col_pad, orders, mode_pad)
    seeds, lines = legendre_seeds(lon_parts, orders, modes, total_degrees, total_rows)

    def each(shape_of):
        return tuple(
            pltpu.VMEM(shape_of(per * LANES, (last - first) * LANES), bf16)
            for first, last, per in groups
        )

    block = each(lambda chunk, width: (lon_parts, mode_pad, chunk))
    column_block = each(lambda chunk, width: (lon_parts, col_pad, chunk))
    return pl.pallas_call(
        functools.partial(block_kernel, lat_parts, lon_parts, groups, modes),
        out_shape=jax.ShapeDtypeStruct((rows, cols, channels), f32),
        in_specs=[hbm] * 9,
        out_specs=vmem,
        scratch_shapes=[
            pltpu.VMEM((rows, cols, channels), f32),
            pltpu.VMEM(norm_gain.shape, f32),
            pltpu.VMEM(degree_keep.shape, degree_keep.dtype),
            pltpu.VMEM(forward.shape, bf16),
            pltpu.VMEM(inverse.shape, bf16),
            pltpu.VMEM(seeds.shape[1:], f32),
            pltpu.VMEM(lines.shape, f32),
            pltpu.VMEM((rows, col_pad, channels), f32),
            pltpu.VMEM((2, 3, (rows + 2) * col_pad, channels), bf16),
            pltpu.VMEM((2, 3, 3, channels, channels), bf16),
            pltpu.VMEM((2, 2, col_rows, channels), f32),
            pltpu.VMEM((2, 2, col_rows, channels), f32),
            pltpu.VMEM((2, 2, col_pad, channels), bf16),
            pltpu.VMEM((2, 4, 8, channels), f32),
            each(lambda chunk, width: (col_pad, lon_parts * chunk)),
            column_block,
            block,
            block,
            each(lambda chunk, width: (lat_parts, rows * modes, width)),
            each(lambda chunk, width: (lat_parts, degrees * modes, width)),
            block,
            block,
            column_block,
            column_block,
            pltpu.VMEM((total_degrees * modes, total_rows), f32),
            pltpu.VMEM((2, degrees * modes, total_rows * modes), bf16),
            pltpu.VMEM((2, total_degrees * modes, rows * modes), bf16),
            pltpu.VMEM((max(rows, degrees) * modes + mode_pad, channels), f32),
            pltpu.VMEM((degrees * modes, channels), f32),
            pltpu.VMEM((degrees, channels, channels), bf16),
            dma((7,)),
            dma((2,)),
            dma(()),
            dma((2, 8)),
            dma((2, 8)),
            dma((4, len(groups), lon_parts - 1)),
            dma((4, len(groups), lon_parts)),
            dma((2, len(groups), lat_parts - 1)),
            dma((2, len(groups), lat_parts - 1)),
        ],
        compiler_params=pltpu.CompilerParams(collective_id=0, has_side_effects=True),
        name="block",
    )(
        grid_state, norm_gain, degree_keep, jnp.asarray(forward), jnp.asarray(inverse),
        jnp.asarray(seeds), jnp.asarray(lines), conv_weight, filter_weight,
    )


def solution(mesh):
    in_specs = (P("lat", "lon", None), P(), P(), P("lat", None, None), P("lat", "lon"))
    out_specs = P("lat", "lon", None)
    return jax.shard_map(
        per_device, mesh=mesh, in_specs=in_specs, out_specs=out_specs, check_vma=False
    )
```
